32 devices in a mesh: groups: 1, rec: 32 (over z, y, x, core).
Axes of the slice: x: 2, y: 2, z: 4, core: 2. Of those that a mesh axis runs over, the one named last changes fastest.
Arguments:
- records: bfloat16 [4, 512, 2, 128], P(None, ('groups', 'rec')), may hold values from -6 to 6
- dest: int32 [512, 4], P('groups'), may hold values from 0 to 31, as said below
- w_in: bfloat16 [64, 36], replicated, may hold values from -1 to 1
- b_in: float32 [64], replicated, may hold values from -3 to 3
- w_mid: bfloat16 [64, 64], replicated, may hold values from -0.75 to 0.75
- b_mid: float32 [64], replicated, may hold values from -3 to 3
- w_out: bfloat16 [64, 36], replicated, may hold values from -0.25 to 0.25
Outputs:
- residual: float32 [4, 512, 2, 128], P(None, ('groups', 'rec'))
- grad_w_in: float32 [64, 36], P('groups')
- grad_b_in: float32 [64], P('groups')
- grad_w_mid: float32 [64, 64], P('groups')
- grad_b_mid: float32 [64], P('groups')
- grad_w_out: float32 [64, 36], P('groups')
The draws below stay inside these ranges and needn't reach their ends.
Inputs may be any that keep to these rules, and one draw needn't show every extreme that they name: `dest`: from the 16 blocks of one record device at most 2 copies go to one owner; in every draw one owner receives exactly 2 copies from every record device.
All inputs are finite; a program needn't handle non-finite values.
Results may differ from the reference program's by a relative error of at most 0.0005.
The reference program's roundings to bfloat16 on the way count: a program that leaves them out, or rounds other values in their place, can miss the bound.
Values may be sent and summed in bfloat16 or wider, within the bound.
A program may use at most 192 MiB of HBM per device.

```python
import math
import jax
import jax.numpy as jnp
from jax import lax

C = 64
CMP = 4
VES = 4
CAP = 2
TR = 2
S = 128
CH = 16
BLOCKS = 512
N_REC = 32


def draw_dest(key, part):
    total = VES * CH
    slots = CAP * N_REC
    key_busy, key_rows = jax.random.split(jax.random.fold_in(key, 17))
    busy = jax.random.randint(key_busy, (), 0, N_REC)
    tokens = jnp.arange(slots, dtype=jnp.int32)
    owner = tokens // CAP

    def one_device(row_key):
        key_score, key_perm = jax.random.split(row_key)
        score = jax.random.randint(key_score, (slots,), 0, 1048576) * slots + tokens
        score = jnp.where(owner == busy, tokens - slots, score)
        order = jnp.argsort(score, stable=True)
        chosen = owner[order[:total]]
        return chosen[jax.random.permutation(key_perm, total)]
    rows = jax.vmap(one_device)(jax.random.split(key_rows, N_REC))
    return rows.reshape(N_REC * CH, VES).astype(jnp.int32)


def steps_of(own_key, dims, pieces, low, high):
    gain = 1.0
    for axis_at, shards_of in pieces:
        draws = jax.random.uniform(jax.random.fold_in(jax.random.fold_in(own_key, 6), axis_at), (shards_of,), jnp.float32, low / len(pieces), high / len(pieces))
        gain = gain * jnp.repeat(jnp.exp(draws), dims[axis_at] // shards_of).reshape((-1,) + (1,) * (len(dims) - 1 - axis_at))
    return gain


def normal_values(stream_key, shape, scale, reach, cuts=(), kind=jnp.bfloat16):
    loudness = steps_of(stream_key, shape, cuts, -0.22, 0.18) if cuts else 1.0
    drawn = jax.random.normal(stream_key, shape, jnp.float32) * scale * loudness
    return jnp.minimum(jnp.maximum(drawn, -reach), reach).astype(kind)


def setup_inputs(seed: int = 0, part: int = 0) -> dict:
    arg_keys = jax.random.split(jax.random.key(seed), 8)
    part_keys = jax.random.split(jax.random.fold_in(arg_keys[7], part), 8)
    return {
        "records": normal_values(part_keys[0], (CMP, BLOCKS, TR, S), 1.0, 6.0, ((1, 32),)),
        "dest": draw_dest(jax.random.fold_in(jax.random.fold_in(arg_keys[7], part), 71), part),
        "w_in": normal_values(arg_keys[2], (C, CMP * 9), (CMP * 9) ** -0.5, 1.0),
        "b_in": normal_values(arg_keys[3], (C,), 0.5, 3.0, (), jnp.float32),
        "w_mid": normal_values(arg_keys[4], (C, C), C ** -0.5, 0.75),
        "b_mid": normal_values(arg_keys[5], (C,), 0.5, 3.0, (), jnp.float32),
        "w_out": normal_values(arg_keys[6], (C, CMP * 9), (C * 9) ** -0.5, 0.25),
    }


def patches(field, flip):
    count, height, width = field.shape
    padded = jnp.pad(field, ((0, 0), (1, 1), (1, 1)))
    taps = []
    for row in range(3):
        for col in range(3):
            top = 2 - row if flip else row
            left = 2 - col if flip else col
            taps.append(padded[:, top:top + height, left:left + width])
    return jnp.stack(taps, axis=1).reshape(count * 9, height, width)

def collect(terms, parts):
    height, width = (terms.shape[1], terms.shape[2])
    stacked = jnp.pad(terms.reshape(parts, 9, height, width), ((0, 0), (0, 0), (1, 1), (1, 1)))
    total = jnp.zeros((parts, height, width), jnp.float32)
    for row in range(3):
        for col in range(3):
            total = total + stacked[:, 3 * row + col, row:row + height, col:col + width]
    return total

def silu_grad(z):
    sig = jax.nn.sigmoid(z)
    return sig * (1.0 + z * (1.0 - sig))

def forward(image, w_in, b_in, w_mid, b_mid, w_out):
    inputs = patches(image, False)
    z1 = jnp.einsum('cu,uhw->chw', w_in.astype(jnp.float32), inputs.astype(jnp.float32)) + b_in[:, None, None]
    a1 = jax.nn.silu(z1).astype(jnp.bfloat16)
    z2 = jnp.einsum('dc,chw->dhw', w_mid.astype(jnp.float32), a1.astype(jnp.float32)) + b_mid[:, None, None]
    a2 = jax.nn.silu(z2).astype(jnp.bfloat16)
    terms = jnp.einsum('cu,chw->uhw', w_out.astype(jnp.float32), a2.astype(jnp.float32))
    estimate = collect(terms, image.shape[0])
    return (estimate, (inputs, z1, a1, z2, a2))

def backward(grad_image, w_mid, w_out, saved):
    inputs, z1, a1, z2, a2 = saved
    flipped = patches(grad_image, True).astype(jnp.float32)
    dw_out = jnp.einsum('chw,uhw->cu', a2.astype(jnp.float32), flipped)
    da2 = jnp.einsum('cu,uhw->chw', w_out.astype(jnp.float32), flipped)
    dz2 = (da2 * silu_grad(z2)).astype(jnp.bfloat16).astype(jnp.float32)
    dw_mid = jnp.einsum('dhw,chw->dc', dz2, a1.astype(jnp.float32))
    db_mid = lax.optimization_barrier(jnp.sum(dz2, axis=(1, 2)))
    da1 = jnp.einsum('dc,dhw->chw', w_mid.astype(jnp.float32), dz2)
    dz1 = (da1 * silu_grad(z1)).astype(jnp.bfloat16).astype(jnp.float32)
    dw_in = jnp.einsum('chw,uhw->cu', dz1, inputs.astype(jnp.float32))
    db_in = lax.optimization_barrier(jnp.sum(dz1, axis=(1, 2)))
    return (dw_in, db_in, dw_mid, db_mid, dw_out)

def reference(records, dest, w_in, b_in, w_mid, b_mid, w_out):
    count = N_REC
    items = CH * VES
    table = dest.reshape(count, items).astype(jnp.int32)
    owners = jnp.arange(count, dtype=jnp.int32)
    sources = jnp.arange(count, dtype=jnp.int32)[:, None] * CH + jnp.arange(items, dtype=jnp.int32)[None, :] // VES
    ranks_k = jnp.arange(CAP, dtype=jnp.int32)

    def owner_index(owner):
        hits = (table == owner).astype(jnp.int32)
        ranks = jnp.cumsum(hits, axis=1) - 1
        chosen = hits[:, None, :] * (ranks[:, None, :] == ranks_k[None, :, None]).astype(jnp.int32)
        pick = lax.optimization_barrier(jnp.sum(chosen * sources[:, None, :], axis=2)).reshape(count * CAP)
        valid = lax.optimization_barrier(jnp.sum(chosen, axis=2)).reshape(count * CAP)
        return (pick.astype(jnp.int32), valid)

    def assemble(field, owner):
        pick, valid = owner_index(owner)
        taken = jnp.take(field, pick, axis=1) * valid.astype(field.dtype)[None, :, None, None]
        return taken.reshape(CMP, count * CAP * TR, S)

    def make_estimate(owner):
        estimate, saved = forward(assemble(records, owner), w_in, b_in, w_mid, b_mid, w_out)
        return estimate.astype(jnp.bfloat16).reshape(CMP, count * CAP, TR, S)
    estimates = lax.map(make_estimate, owners)
    hits3 = (table[:, :, None] == owners[None, None, :]).astype(jnp.int32)
    rank = lax.optimization_barrier(jnp.sum((jnp.cumsum(hits3, axis=1) - 1) * hits3, axis=2))
    slot = (jnp.arange(count, dtype=jnp.int32)[:, None] * CAP + rank).reshape(-1).astype(jnp.int32)
    values = estimates[table.reshape(-1), :, slot]
    values = values.astype(jnp.float32).reshape(count, CH, VES, CMP, TR, S)
    reblend = lax.optimization_barrier(jnp.sum(values, axis=2)).reshape(count * CH, CMP, TR, S)
    reblend = jnp.transpose(reblend, (1, 0, 2, 3))
    residual = reblend - records.astype(jnp.float32)
    rounded = residual.astype(jnp.bfloat16)

    def owner_grads(owner):
        estimate, saved = forward(assemble(records, owner), w_in, b_in, w_mid, b_mid, w_out)
        return backward(assemble(rounded, owner), w_mid, w_out, saved)
    terms = lax.map(owner_grads, owners)
    scale = 1.0 / math.sqrt(CMP * BLOCKS * TR * S)
    grads = tuple((lax.optimization_barrier(jnp.sum(term, axis=0)) * scale for term in terms))
    return (residual, grads[0], grads[1], grads[2], grads[3], grads[4])
```

```python
import functools
import math

import jax
import jax.numpy as jnp
from jax import lax
from jax.experimental import pallas as pl
from jax.experimental.pallas import tpu as pltpu
from jax.sharding import PartitionSpec as P

VES = 4
F32 = jnp.float32
BF16 = jnp.bfloat16
NT = (((1,), (1,)), ((), ()))
TN = (((0,), (0,)), ((), ()))
MESH = pl.DeviceIdType.MESH

OWN, FIELD = 64, 112
GROUPS = ((1, 2), (0, 3), (-1, 4))


def iota(shape, dim):
    return lax.broadcasted_iota(jnp.int32, shape, dim)


def dot(a, b, dims=None):
    if dims is None:
        return jnp.dot(a, b, preferred_element_type=F32)
    return lax.dot_general(a, b, dims, preferred_element_type=F32)


def onehot(mask, value=1.0):
    return jnp.where(mask, value, 0.0).astype(F32)


def tap_of(k, q, flip):
    inner = k & 63
    col, trace, comp = inner >> 4, (inner >> 2) & 3, inner & 3
    at = jnp.where(k < OWN, trace, jnp.where(trace < 2, trace - 2, trace + 2))
    row = at - q + 1
    ok = (row >= 0) & (row <= 2) & (col <= 2) & (k < FIELD)
    if flip:
        row, col = 2 - row, 2 - col
    return jnp.where(ok, 9 * comp + 3 * row + col, -1)


def split3(x):
    high = x.astype(BF16)
    rest = x - high.astype(F32)
    middle = rest.astype(BF16)
    low = (rest - middle.astype(F32)).astype(BF16)
    return high, middle, low


def kernel(
    n, scale, chunk,
    rec_ref, dest_ref, w_in_ref, b_in_ref, w_mid_ref, b_mid_ref, w_out_ref,
    res_ref, grad_ref,
    halo, mine, qhalo, parts, in4, part, in5,
    sel, sel_t, sel_h, w1, w2, w3, wm, wm_t, fold,
    xs, qs, est, a1s, a2s, d1s, d2s, g1, g2, gm,
    near_send, near_recv, send_sem, recv_sem,
):
    me = lax.axis_index("rec")
    blocks = rec_ref.shape[0] // 8
    low, high = me > 0, me < n - 1

    barrier = pltpu.get_barrier_semaphore()

    def greet(d, _):
        pl.semaphore_signal(
            barrier, inc=1, device_id={"rec": (me + d) % n}, device_id_type=MESH
        )
        return 0

    lax.fori_loop(1, n, greet, 0, unroll=True)

    def to_neighbour(src, dst, phase, up):
        return pltpu.make_async_remote_copy(
            src_ref=src,
            dst_ref=dst.at[pl.ds(0 if up else 128, 128)],
            send_sem=near_send.at[2 * phase + up],
            recv_sem=near_recv.at[2 * phase + up],
            device_id={"rec": me + 1 if up else me - 1},
            device_id_type=MESH,
        )

    def swap(src, dst, phase):
        @pl.when(high)
        def _():
            to_neighbour(src, dst, phase, 1).start()

        @pl.when(low)
        def _():
            to_neighbour(src, dst, phase, 0).start()

    def swapped(src, dst, phase):
        @pl.when(low)
        def _():
            to_neighbour(src, dst, phase, 1).wait_recv()

        @pl.when(high)
        def _():
            to_neighbour(src, dst, phase, 0).wait_recv()

    def swap_sent(src, dst, phase):
        @pl.when(high)
        def _():
            to_neighbour(src, dst, phase, 1).wait_send()

        @pl.when(low)
        def _():
            to_neighbour(src, dst, phase, 0).wait_send()

    @pl.when(me == 0)
    def _():
        for ref in (halo, qhalo):
            ref[0:128] = jnp.zeros((128, 128), BF16)

    @pl.when(me == n - 1)
    def _():
        for ref in (halo, qhalo):
            ref[128:256] = jnp.zeros((128, 128), BF16)

    column = iota((blocks, 128), 1)
    item = (column >> 1) % blocks
    block = iota((blocks, 128), 0)
    length = dest_ref.shape[1]
    lane = iota((1, 128), 1)
    inner = (lane & 1) * 4 + (lane >> 5)
    rows = iota((16 * n, 128), 0)

    def targets(source):
        wanted = iota((blocks, length), 1) - iota((blocks, length), 0) == source * blocks
        here = [
            jnp.broadcast_to(
                jnp.sum(jnp.where(wanted, dest_ref[v : v + 1], 0), axis=1, keepdims=True), (blocks, 128)
            )
            for v in range(VES)
        ]
        found = []
        for v in range(VES):
            own = jnp.sum(jnp.where(block == item, here[v], 0), axis=0, keepdims=True)
            rank = jnp.zeros((blocks, 128), jnp.int32)
            for u in range(VES):
                before = (block <= item) if u < v else (block < item)
                rank = rank + jnp.where(before & (here[u] == own), 1, 0)
            found.append((own, jnp.sum(rank, axis=0, keepdims=True)))
        return found

    def matches(targets_):
        mask = None
        for target in targets_:
            hit = rows == target
            mask = hit if mask is None else mask | hit
        return onehot(mask)

    picked = matches([own * 16 + rank * 8 + inner for own, rank in targets(me)])
    sel[...] = picked.astype(BF16)
    sel_t[...] = picked.T.astype(BF16)
    before = [
        jnp.where((rank == 1) & low, own * 16 + inner, -1) for own, rank in targets(me - 1)
    ]
    after = [
        jnp.where((rank == 0) & high, own * 16 + 8 + inner, -1) for own, rank in targets(me + 1)
    ]
    sel_h[:, 0:128] = matches(before).astype(BF16)
    sel_h[:, 128:256] = matches(after).astype(BF16)

    pl.semaphore_wait(barrier, n - 1)
    swap(rec_ref, halo, 0)

    u = iota((36, 128), 0)
    k = iota((36, 128), 1)
    bias_at = iota((128, 128), 1) - 48
    near = (iota((128, 64), 0) & 63) == iota((128, 64), 1)

    def bias_of(b_ref, at, base):
        values = jnp.sum(jnp.where(near, 0.5 * b_ref[...], 0.0), axis=1, keepdims=True)
        out = base
        for i, piece in enumerate(split3(values)):
            out = out + jnp.where(at == i, piece.astype(F32), 0.0)
        return out

    for g, qs_ in enumerate(GROUPS):
        pair = jnp.concatenate(
            [dot(w_in_ref[...], onehot(u == tap_of(k, q, False), 0.5).astype(BF16), TN) for q in qs_], axis=0
        )
        w1[g] = bias_of(b_in_ref, bias_at, pair).astype(BF16)
        w3[:, 128 * g : 128 * g + 128] = jnp.concatenate(
            [
                dot(onehot(u[:, 0:48] == tap_of(k[:, 0:48], q, True)).astype(BF16), w_out_ref[...], TN)
                for q in qs_
            ],
            axis=1,
        ).astype(BF16)
        if g < 2:
            w2[g] = jnp.concatenate(
                [dot(w_out_ref[...], onehot(u == tap_of(k, q, True), 0.5).astype(BF16), TN) for q in qs_], axis=0
            ).astype(BF16)
    outer = iota((48, 128), 1)
    inside_ = ((outer >= 64) | low) & ((outer < 64) | high)
    w3[:, 256:384] = jnp.where(inside_, w3[:, 256:384].astype(F32), 0.0).astype(BF16)
    wide = onehot((iota((64, 128), 1) & 63) == iota((64, 128), 0), 0.5).astype(BF16)
    half = dot(w_mid_ref[...], wide)
    diagonal = iota((128, 128), 0) >> 6 == iota((128, 128), 1) >> 6
    once = jnp.where(diagonal, jnp.concatenate([half, half], axis=0), 0.0)
    wm[:, 0:128] = once.astype(BF16)
    wm[:, 128:144] = bias_of(b_mid_ref, iota((128, 16), 1), jnp.zeros((128, 16), F32)).astype(BF16)
    wm_t[...] = once.T.astype(BF16)

    sample = iota((128, 128), 1)

    def taps(x):
        x = x.astype(F32)
        left = jnp.where(sample > 0, pltpu.roll(x, 1, 1), 0.0)
        right = jnp.where(sample < 127, pltpu.roll(x, 127, 1), 0.0)
        return jnp.concatenate([left.astype(BF16), x.astype(BF16), right.astype(BF16)], axis=1)

    def spread(choose, source, field, start):
        def step(c, _):
            tiles = dot(choose[pl.ds(pl.multiple_of(c * 128, 128), 128)], source).astype(BF16)
            for t in range(8):
                at = pl.ds(pl.multiple_of((c * 8 + t) * 128, 128), 128)
                for j in range(3):
                    field[start + 16 * j : start + 16 * j + 16, at] = tiles[
                        16 * t : 16 * t + 16, 128 * j : 128 * j + 128
                    ]
            return 0

        lax.fori_loop(0, n // 8, step, 0, unroll=4)

    spread(sel, taps(rec_ref[...]), xs, 0)
    ones = onehot(iota((16, n * 128), 0) < 3).astype(BF16)
    xs[48:64] = ones
    qs[48:64] = jnp.zeros((16, n * 128), BF16)

    size = chunk * 128
    const = onehot(iota((16, size), 0) < 3).astype(BF16)

    def activate(h):
        up = 1.0 + jnp.tanh(h)
        a = h * up
        return a.astype(BF16), up, a

    def hidden(g, depth, at):
        a1, up, a = activate(dot(w1[g, :, 0:depth], xs[0:depth, at]))
        if g < 2:
            a1s[g, :, at] = a1
            d1s[g, :, at] = up + a * (2.0 - up)
        a2, up, a = activate(dot(wm[...], jnp.concatenate([a1, const], axis=0)))
        if g < 2:
            a2s[g, :, at] = a2
            d2s[g, :, at] = up + a * (2.0 - up)
        return a2

    def inside(c, _):
        hidden(0, OWN, pl.ds(pl.multiple_of(c * size, 128), size))
        return 0

    lax.fori_loop(0, n // chunk, inside, 0)

    swapped(rec_ref, halo, 0)
    spread(sel_h, jnp.concatenate([taps(halo[0:128]), taps(halo[128:256])], axis=0), xs, OWN)

    small = iota((16, 128), 1)

    def border(c, _):
        at = pl.ds(pl.multiple_of(c * size, 128), size)
        a2 = jnp.concatenate([a2s[0, :, at], hidden(1, FIELD, at), hidden(2, FIELD, at)], axis=0)
        terms = dot(w3[...], a2)
        for t in range(chunk):
            x = terms[:, 128 * t : 128 * t + 128]
            first = jnp.where(small < 127, pltpu.roll(x[0:16], 127, 1), 0.0)
            last = jnp.where(small > 0, pltpu.roll(x[32:48], 1, 1), 0.0)
            est[c * chunk + t] = (x[16:32] + first + last).astype(BF16)
        return 0

    lax.fori_loop(0, n // chunk, border, 0)

    residual = dot(sel_t[...], est[...].reshape(16 * n, 128)) - rec_ref[...].astype(F32)
    res_ref[...] = residual
    mine[...] = residual.astype(BF16)
    swap(mine, qhalo, 1)

    spread(sel, taps(mine[...]), qs, 0)
    for g in (g1, g2, gm):
        g[...] = jnp.zeros_like(g)
    u = iota((128, 128), 0)
    k = iota((128, 128), 1)
    for i, q in enumerate(GROUPS[0] + GROUPS[1]):
        tap = tap_of(k, q, False)
        fold[:, 128 * i : 128 * i + 128] = onehot((u == tap) | ((k == 48) & (u == 36))).astype(BF16)
        tap = tap_of(k, q, True)
        fold[:, 512 + 128 * i : 640 + 128 * i] = onehot((u - 64 == tap) & (tap >= 0)).astype(BF16)
    for i in range(2):
        fold[:, 1024 + 128 * i : 1152 + 128 * i] = onehot((k == 0) & (u == 37)).astype(BF16)

    def backward(g, depth):
        def step(c, _):
            at = pl.ds(pl.multiple_of(c * size, 128), size)
            row = slice(128 * g, 128 * g + 128)
            field = qs[0:depth, at]
            g2[row, 0:depth] += dot(a2s[g, :, at], field, NT)
            dz2 = (dot(w2[g, :, 0:depth], field) * d2s[g, :, at]).astype(BF16)
            gm[:, 0:144] += dot(dz2, jnp.concatenate([a1s[g, :, at], const], axis=0), NT)
            dz1 = (dot(wm_t[...], dz2) * d1s[g, :, at]).astype(BF16)
            g1[row, 0:depth] += dot(dz1, xs[0:depth, at], NT)
            return 0

        lax.fori_loop(0, n // chunk, step, 0)

    backward(0, OWN)
    swapped(mine, qhalo, 1)
    spread(sel_h, jnp.concatenate([taps(qhalo[0:128]), taps(qhalo[128:256])], axis=0), qs, OWN)
    backward(1, FIELD)

    pieces = [g[64 * i : 64 * i + 64] for g in (g1, g2) for i in range(4)]
    pieces += [gm[0:64, 128:256], gm[64:128, 128:256]]
    total = None
    for piece in split3(jnp.concatenate(pieces, axis=1)):
        term = dot(fold[...], piece, NT)
        total = term if total is None else total + term
    total = jnp.concatenate([total, jnp.zeros((128, 64), F32)], axis=1)
    square = pltpu.roll(gm[0:64, 0:128], 64, 1) + gm[64:128, 0:128]
    square = jnp.where(iota((64, 128), 1) >= 64, square, 0.0)
    total = [total[0:64] + square, total[64:128]]
    per = 128 // n
    for i in range(n):
        start = (i * per) % 64
        parts[i] = total[i * per // 64][start : start + per]

    def send(src_of, dst, phase):
        def step(d, _):
            peer = (me + d) % n
            pltpu.make_async_remote_copy(
                src_ref=src_of(peer),
                dst_ref=dst.at[me],
                send_sem=send_sem.at[phase],
                recv_sem=recv_sem.at[phase],
                device_id={"rec": peer},
                device_id_type=MESH,
            ).start()
            return 0

        lax.fori_loop(1, n, step, 0, unroll=True)

    def wait(ref, sem):
        every = ref.at[pl.ds(0, n - 1)]
        pltpu.make_async_copy(every, every, sem).wait()

    send(lambda peer: parts.at[peer], in4, 0)
    in4[me] = parts[me]
    wait(in4, recv_sem.at[0])
    part[...] = jnp.sum(in4[...], axis=0, keepdims=True) * scale
    send(lambda peer: part.at[0], in5, 1)
    in5[me] = part[0]
    wait(in5, recv_sem.at[1])
    for i in range(n):
        grad_ref[per * i : per * i + per] = in5[i]
    swap_sent(rec_ref, halo, 0)
    swap_sent(mine, qhalo, 1)
    wait(parts, send_sem.at[0])
    wait(in5, send_sem.at[1])


def deal(res_ref, grad_ref, out_ref, dwi_ref, dbi_ref, dwm_ref, dbm_ref, dwo_ref):
    out_ref[...] = res_ref[...]
    dwi_ref[...] = grad_ref[0:36, 0:64]
    dbi_ref[...] = grad_ref[36:37, 0:64]
    dbm_ref[...] = grad_ref[37:38, 0:64]
    dwo_ref[...] = grad_ref[64:100, 0:64]
    dwm_ref[...] = pltpu.roll(grad_ref[0:64], 64, 1)[:, 0:64]


def local(n, records, dest, w_in, b_in, w_mid, b_mid, w_out):
    parts, blocks, traces, samples = records.shape
    width = n * samples
    per = 128 // n
    chunk = max(4, 512 // n)
    scale = 1.0 / math.sqrt(parts * blocks * n * traces * samples)
    vmem = pl.BlockSpec(memory_space=pltpu.VMEM)
    V = pltpu.VMEM
    piece = V((n, per, 128), F32)
    result = pl.pallas_call(
        functools.partial(kernel, n, scale, chunk),
        out_shape=(
            jax.ShapeDtypeStruct((128, 128), F32),
            jax.ShapeDtypeStruct((128, 128), F32),
        ),
        in_specs=[vmem] * 7,
        out_specs=(vmem,) * 2,
        scratch_shapes=[
            V((256, 128), BF16), V((128, 128), BF16), V((256, 128), BF16),
            piece, piece, V((1, per, 128), F32), piece,
            V((16 * n, 128), BF16), V((128, 16 * n), BF16), V((16 * n, 256), BF16),
            V((3, 128, 128), BF16), V((2, 128, 128), BF16), V((48, 384), BF16),
            V((128, 144), BF16), V((128, 128), BF16), V((128, 1280), BF16),
            V((FIELD, width), BF16), V((FIELD, width), BF16), V((n, 16, 128), BF16),
            V((2, 128, width), BF16), V((2, 128, width), BF16),
            V((2, 128, width), F32), V((2, 128, width), F32),
            V((256, 128), F32), V((256, 128), F32), V((128, 256), F32),
            pltpu.SemaphoreType.DMA((4,)), pltpu.SemaphoreType.DMA((4,)),
            pltpu.SemaphoreType.DMA((2,)), pltpu.SemaphoreType.DMA((2,)),
        ],
        compiler_params=pltpu.CompilerParams(
            collective_id=0, has_side_effects=True, vmem_limit_bytes=63 << 20
        ),
        name="deblend",
    )(
        records.reshape(128, 128), dest.T, w_in.T, b_in.reshape(1, 64), w_mid, b_mid.reshape(1, 64), w_out.T
    )
    residual, dwi, dbi, dwm, dbm, dwo = pl.pallas_call(
        deal,
        out_shape=(
            jax.ShapeDtypeStruct((128, 128), F32),
            jax.ShapeDtypeStruct((36, 64), F32),
            jax.ShapeDtypeStruct((1, 64), F32),
            jax.ShapeDtypeStruct((64, 64), F32),
            jax.ShapeDtypeStruct((1, 64), F32),
            jax.ShapeDtypeStruct((36, 64), F32),
        ),
        in_specs=[vmem] * 2,
        out_specs=(vmem,) * 6,
        name="deal",
    )(*result)
    return (
        residual.reshape(records.shape),
        dwi.T,
        dbi.reshape(64),
        dwm,
        dbm.reshape(64),
        dwo.T,
    )


def solution(mesh):
    return jax.shard_map(
        functools.partial(local, mesh.shape["rec"]),
        mesh=mesh,
        in_specs=(
            P(None, ("groups", "rec"), None, None),
            P("groups", None),
            P(),
            P(),
            P(),
            P(),
            P(),
        ),
        out_specs=(
            P(None, ("groups", "rec"), None, None),
            P("groups", None),
            P("groups"),
            P("groups", None),
            P("groups"),
            P("groups", None),
        ),
        check_vma=False,
    )
```

```python
import functools
import math

import jax
import jax.numpy as jnp
from jax import lax
from jax.experimental import pallas as pl
from jax.experimental.pallas import tpu as pltpu
from jax.sharding import PartitionSpec as P

VES = 4
F32 = jnp.float32
BF16 = jnp.bfloat16
NT = (((1,), (1,)), ((), ()))
TN = (((0,), (0,)), ((), ()))
MESH = pl.DeviceIdType.MESH

OWN, FIELD = 64, 112
GROUPS = ((1, 2), (0, 3), (-1, 4))


def iota(shape, dim):
    return lax.broadcasted_iota(jnp.int32, shape, dim)


def dot(a, b, dims=None):
    if dims is None:
        return jnp.dot(a, b, preferred_element_type=F32)
    return lax.dot_general(a, b, dims, preferred_element_type=F32)


def onehot(mask, value=1.0):
    return jnp.where(mask, value, 0.0).astype(F32)


def tap_of(k, q, flip):
    inner = k & 63
    col, trace, comp = inner >> 4, (inner >> 2) & 3, inner & 3
    at = jnp.where(k < OWN, trace, jnp.where(trace < 2, trace - 2, trace + 2))
    row = at - q + 1
    ok = (row >= 0) & (row <= 2) & (col <= 2) & (k < FIELD)
    if flip:
        row, col = 2 - row, 2 - col
    return jnp.where(ok, 9 * comp + 3 * row + col, -1)


def split3(x):
    high = x.astype(BF16)
    rest = x - high.astype(F32)
    middle = rest.astype(BF16)
    low = (rest - middle.astype(F32)).astype(BF16)
    return high, middle, low


def kernel(
    n, scale, chunk,
    rec_hbm, dest_hbm, w_in_hbm, b_in_hbm, w_mid_hbm, b_mid_hbm, w_out_hbm,
    res_ref, grad_ref,
    rec_ref, dest_ref, w_in_ref, b_in_ref, w_mid_ref, b_mid_ref, w_out_ref,
    halo, mine, qhalo, packed, parts, in4, part, in5,
    sel, sel_t, sel_h, w1, w2, w3, wm, wm_t, fold1, fold2,
    xs, qs, est, a1s, a2s, d1s, d2s, g1, g2, gm,
    load_sem, near_send, near_recv, send_sem, recv_sem, entered,
):
    me = lax.axis_index("rec")
    blocks = rec_ref.shape[0] // 8
    low, high = me > 0, me < n - 1
    group = n // 2
    plane = 8
    planes = n // plane

    barrier = pltpu.get_barrier_semaphore()
    here = (me // plane) * plane
    place = me - here

    def greet(sem, peer):
        pl.semaphore_signal(sem, inc=1, device_id={"rec": peer}, device_id_type=MESH)

    up_out = high & (place == plane - 1)
    down_out = low & (place == 0)

    @pl.when(up_out)
    def _():
        greet(barrier, me + 1)

    @pl.when(down_out)
    def _():
        greet(barrier, me - 1)

    for d in range(1, plane):
        greet(barrier, here + (place + d) % plane)
    for d in range(1, planes):
        greet(barrier, (me + d * plane) % n)

    loads = [
        pltpu.make_async_copy(src, dst, load_sem.at[i])
        for i, (src, dst) in enumerate(
            (
                (dest_hbm, dest_ref), (rec_hbm, rec_ref), (w_in_hbm, w_in_ref), (b_in_hbm, b_in_ref),
                (w_mid_hbm, w_mid_ref), (b_mid_hbm, b_mid_ref), (w_out_hbm, w_out_ref),
            )
        )
    ]
    for load in loads:
        load.start()

    def to_neighbour(src, dst, phase, up):
        return pltpu.make_async_remote_copy(
            src_ref=src,
            dst_ref=dst.at[pl.ds(0 if up else 128, 128)],
            send_sem=near_send.at[2 * phase + up],
            recv_sem=near_recv.at[2 * phase + up],
            device_id={"rec": me + 1 if up else me - 1},
            device_id_type=MESH,
        )

    def swap(src, dst, phase):
        @pl.when(high)
        def _():
            to_neighbour(src, dst, phase, 1).start()

        @pl.when(low)
        def _():
            to_neighbour(src, dst, phase, 0).start()

    def swapped(src, dst, phase):
        @pl.when(low)
        def _():
            to_neighbour(src, dst, phase, 1).wait_recv()

        @pl.when(high)
        def _():
            to_neighbour(src, dst, phase, 0).wait_recv()

    def swap_sent(src, dst, phase):
        @pl.when(high)
        def _():
            to_neighbour(src, dst, phase, 1).wait_send()

        @pl.when(low)
        def _():
            to_neighbour(src, dst, phase, 0).wait_send()

    @pl.when(me == 0)
    def _():
        for ref in (halo, qhalo):
            ref[0:128] = jnp.zeros((128, 128), BF16)

    @pl.when(me == n - 1)
    def _():
        for ref in (halo, qhalo):
            ref[128:256] = jnp.zeros((128, 128), BF16)

    column = iota((blocks, 128), 1)
    item = (column >> 1) % blocks
    block = iota((blocks, 128), 0)
    length = dest_ref.shape[1]
    lane = iota((1, 128), 1)
    inner = (lane & 1) * 4 + (lane >> 5)
    rows = iota((16 * n, 128), 0)

    loads[0].wait()

    def targets(source):
        wanted = iota((blocks, length), 1) - iota((blocks, length), 0) == source * blocks
        dests = [
            jnp.broadcast_to(
                jnp.sum(jnp.where(wanted, dest_ref[v : v + 1], 0), axis=1, keepdims=True), (blocks, 128)
            )
            for v in range(VES)
        ]
        found = []
        for v in range(VES):
            own = jnp.sum(jnp.where(block == item, dests[v], 0), axis=0, keepdims=True)
            rank = jnp.zeros((blocks, 128), jnp.int32)
            for u in range(VES):
                before = (block <= item) if u < v else (block < item)
                rank = rank + jnp.where(before & (dests[u] == own), 1, 0)
            found.append((own, jnp.sum(rank, axis=0, keepdims=True)))
        return found

    def matches(targets_):
        mask = None
        for target in targets_:
            hit = rows == target
            mask = hit if mask is None else mask | hit
        return onehot(mask)

    picked = matches([own * 16 + rank * 8 + inner for own, rank in targets(me)])
    sel[...] = picked.astype(BF16)
    sel_t[...] = picked.T.astype(BF16)
    before = [
        jnp.where((rank == 1) & low, own * 16 + inner, -1) for own, rank in targets(me - 1)
    ]
    after = [
        jnp.where((rank == 0) & high, own * 16 + 8 + inner, -1) for own, rank in targets(me + 1)
    ]
    sel_h[:, 0:128] = matches(before).astype(BF16)
    sel_h[:, 128:256] = matches(after).astype(BF16)

    loads[1].wait()
    pl.semaphore_wait(
        barrier, plane + planes - 2 + jnp.where(up_out, 1, 0) + jnp.where(down_out, 1, 0)
    )
    swap(rec_ref, halo, 0)
    for d in range(1, planes):
        greet(entered, (me + d * plane) % n)
    for load in loads[2:]:
        load.wait()

    u = iota((36, 128), 0)
    k = iota((36, 128), 1)
    bias_at = iota((128, 128), 1) - 48
    near = (iota((128, 64), 0) & 63) == iota((128, 64), 1)

    def bias_of(b_ref, at, base):
        values = jnp.sum(jnp.where(near, 0.5 * b_ref[...], 0.0), axis=1, keepdims=True)
        out = base
        for i, piece in enumerate(split3(values)):
            out = out + jnp.where(at == i, piece.astype(F32), 0.0)
        return out

    for g, qs_ in enumerate(GROUPS):
        pair = jnp.concatenate(
            [dot(w_in_ref[...], onehot(u == tap_of(k, q, False), 0.5).astype(BF16), TN) for q in qs_], axis=0
        )
        w1[g] = bias_of(b_in_ref, bias_at, pair).astype(BF16)
        w3[:, 128 * g : 128 * g + 128] = jnp.concatenate(
            [
                dot(onehot(u[:, 0:48] == tap_of(k[:, 0:48], q, True)).astype(BF16), w_out_ref[...], TN)
                for q in qs_
            ],
            axis=1,
        ).astype(BF16)
        if g < 2:
            w2[g] = jnp.concatenate(
                [dot(w_out_ref[...], onehot(u == tap_of(k, q, True), 0.5).astype(BF16), TN) for q in qs_], axis=0
            ).astype(BF16)
    outer = iota((48, 128), 1)
    inside_ = ((outer >= 64) | low) & ((outer < 64) | high)
    w3[:, 256:384] = jnp.where(inside_, w3[:, 256:384].astype(F32), 0.0).astype(BF16)
    wide = onehot((iota((64, 128), 1) & 63) == iota((64, 128), 0), 0.5).astype(BF16)
    half = dot(w_mid_ref[...], wide)
    diagonal = iota((128, 128), 0) >> 6 == iota((128, 128), 1) >> 6
    once = jnp.where(diagonal, jnp.concatenate([half, half], axis=0), 0.0)
    wm[:, 0:128] = once.astype(BF16)
    wm[:, 128:144] = bias_of(b_mid_ref, iota((128, 16), 1), jnp.zeros((128, 16), F32)).astype(BF16)
    wm_t[...] = once.T.astype(BF16)

    sample = iota((128, 128), 1)

    def taps(x):
        x = x.astype(F32)
        left = jnp.where(sample > 0, pltpu.roll(x, 1, 1), 0.0)
        right = jnp.where(sample < 127, pltpu.roll(x, 127, 1), 0.0)
        return jnp.concatenate([left.astype(BF16), x.astype(BF16), right.astype(BF16)], axis=1)

    def spread(choose, source, field, start):
        def step(c, _):
            tiles = dot(choose[pl.ds(pl.multiple_of(c * 128, 128), 128)], source).astype(BF16)
            for t in range(8):
                at = pl.ds(pl.multiple_of((c * 8 + t) * 128, 128), 128)
                for j in range(3):
                    field[start + 16 * j : start + 16 * j + 16, at] = tiles[
                        16 * t : 16 * t + 16, 128 * j : 128 * j + 128
                    ]
            return 0

        lax.fori_loop(0, n // 8, step, 0, unroll=4)

    spread(sel, taps(rec_ref[...]), xs, 0)
    ones = onehot(iota((16, n * 128), 0) < 3).astype(BF16)
    xs[48:64] = ones
    qs[48:64] = jnp.zeros((16, n * 128), BF16)

    size = chunk * 128
    const = onehot(iota((16, size), 0) < 3).astype(BF16)

    def activate(h):
        up = 1.0 + jnp.tanh(h)
        a = h * up
        return a.astype(BF16), up, a

    def hidden(g, depth, at):
        a1, up, a = activate(dot(w1[g, :, 0:depth], xs[0:depth, at]))
        if g < 2:
            a1s[g, :, at] = a1
            d1s[g, :, at] = up + a * (2.0 - up)
        a2, up, a = activate(dot(wm[...], jnp.concatenate([a1, const], axis=0)))
        if g < 2:
            a2s[g, :, at] = a2
            d2s[g, :, at] = up + a * (2.0 - up)
        return a2

    def inside(c, _):
        hidden(0, OWN, pl.ds(pl.multiple_of(c * size, 128), size))
        return 0

    lax.fori_loop(0, n // chunk, inside, 0)

    swapped(rec_ref, halo, 0)
    spread(sel_h, jnp.concatenate([taps(halo[0:128]), taps(halo[128:256])], axis=0), xs, OWN)

    small = iota((16, 128), 1)

    def border(c, _):
        at = pl.ds(pl.multiple_of(c * size, 128), size)
        a2 = jnp.concatenate([a2s[0, :, at], hidden(1, FIELD, at), hidden(2, FIELD, at)], axis=0)
        terms = dot(w3[...], a2)
        for t in range(chunk):
            x = terms[:, 128 * t : 128 * t + 128]
            first = jnp.where(small < 127, pltpu.roll(x[0:16], 127, 1), 0.0)
            last = jnp.where(small > 0, pltpu.roll(x[32:48], 1, 1), 0.0)
            est[c * chunk + t] = (x[16:32] + first + last).astype(BF16)
        return 0

    lax.fori_loop(0, n // chunk, border, 0)

    residual = dot(sel_t[...], est[...].reshape(16 * n, 128)) - rec_ref[...].astype(F32)
    res_ref[...] = residual
    mine[...] = residual.astype(BF16)
    swap(mine, qhalo, 1)

    spread(sel, taps(mine[...]), qs, 0)
    for g in (g1, g2, gm):
        g[...] = jnp.zeros_like(g)
    u = iota((48, 128), 0)
    k = iota((48, 128), 1)
    for i, q in enumerate(GROUPS[0] + GROUPS[1]):
        at = slice(128 * i, 128 * i + 128)
        fold1[:, at] = onehot((u == tap_of(k, q, False)) | ((k == 48) & (u == 36))).astype(BF16)
        fold2[:, at] = onehot(u == tap_of(k, q, True)).astype(BF16)
    for i in range(2):
        fold2[:, 512 + 128 * i : 640 + 128 * i] = onehot((k == 0) & (u == 36)).astype(BF16)

    def backward(g, depth):
        def step(c, _):
            at = pl.ds(pl.multiple_of(c * size, 128), size)
            row = slice(128 * g, 128 * g + 128)
            field = qs[0:depth, at]
            g2[row, 0:depth] += dot(a2s[g, :, at], field, NT)
            dz2 = (dot(w2[g, :, 0:depth], field) * d2s[g, :, at]).astype(BF16)
            gm[:, 0:144] += dot(dz2, jnp.concatenate([a1s[g, :, at], const], axis=0), NT)
            dz1 = (dot(wm_t[...], dz2) * d1s[g, :, at]).astype(BF16)
            g1[row, 0:depth] += dot(dz1, xs[0:depth, at], NT)
            return 0

        lax.fori_loop(0, n // chunk, step, 0)

    backward(0, OWN)
    swapped(mine, qhalo, 1)
    spread(sel_h, jnp.concatenate([taps(qhalo[0:128]), taps(qhalo[128:256])], axis=0), qs, OWN)
    backward(1, FIELD)

    def folded(fold, pieces):
        total = None
        for piece in split3(jnp.concatenate(pieces, axis=1)):
            term = dot(fold[...], piece, NT)
            total = term if total is None else total + term
        return total

    four = [slice(64 * i, 64 * i + 64) for i in range(4)]
    first = folded(fold1, [g1[at] for at in four])
    second = folded(fold2, [g2[at] for at in four] + [gm[0:64, 128:256], gm[64:128, 128:256]])
    packed[0:40] = jnp.concatenate([first[0:40], second[0:40]], axis=1)
    square = gm[0:64, 0:128] + pltpu.roll(gm[64:128, 0:128], 64, 1)
    packed[40:72] = jnp.where(iota((32, 128), 1) < 64, square[0:32], pltpu.roll(square[32:64], 64, 1))
    packed[72:] = jnp.zeros((packed.shape[0] - 72, 128), F32)
    per = parts.shape[1]
    for i in range(group):
        parts[i] = packed[per * i : per * i + per]

    def send(src, dst, phase, peer):
        pltpu.make_async_remote_copy(
            src_ref=src,
            dst_ref=dst,
            send_sem=send_sem.at[phase],
            recv_sem=recv_sem.at[phase],
            device_id={"rec": peer},
            device_id_type=MESH,
        ).start()

    def wait(ref, count, sem):
        every = ref.at[pl.ds(0, count)]
        pltpu.make_async_copy(every, every, sem).wait()

    base = (me // group) * group
    index = me - base
    pl.semaphore_wait(entered, planes - 1)
    for d in range(group - 1, 0, -1):
        to = (index + d) % group
        send(parts.at[to], in4.at[index], 0, base + to)
    in4[index] = parts[index]
    wait(in4, group - 1, recv_sem.at[0])
    part[...] = jnp.sum(in4[...], axis=0, keepdims=True) * scale
    for d in range(n - 1, 0, -1):
        send(part.at[0], in5.at[me], 1, (me + d) % n)
    in5[me] = part[0]
    wait(in5, n - 1, recv_sem.at[1])
    for i in range(group):
        grad_ref[per * i : per * i + per] = in5[i] + in5[i + group]
    swap_sent(rec_ref, halo, 0)
    swap_sent(mine, qhalo, 1)
    wait(parts, group - 1, send_sem.at[0])
    wait(in5, n - 1, send_sem.at[1])


def deal(res_ref, grad_ref, out_ref, dwi_ref, dbi_ref, dwm_ref, dbm_ref, dwo_ref):
    out_ref[...] = res_ref[...]
    dwi_ref[...] = grad_ref[0:36, 0:64]
    dbi_ref[...] = grad_ref[36:37, 0:64]
    dwm_ref[0:32] = grad_ref[40:72, 0:64]
    dwo_ref[...] = pltpu.roll(grad_ref[0:40], 64, 1)[0:36, 0:64]
    dbm_ref[...] = pltpu.roll(grad_ref[0:40], 64, 1)[36:37, 0:64]
    dwm_ref[32:64] = pltpu.roll(grad_ref[40:72], 64, 1)[:, 0:64]


def local(n, records, dest, w_in, b_in, w_mid, b_mid, w_out):
    parts, blocks, traces, samples = records.shape
    width = n * samples
    group = n // 2
    per = -(-72 // group)
    chunk = min(n, max(4, 1024 // n))
    scale = 1.0 / math.sqrt(parts * blocks * n * traces * samples)
    vmem = pl.BlockSpec(memory_space=pltpu.VMEM)
    V = pltpu.VMEM
    hbm = pl.BlockSpec(memory_space=pl.ANY)
    every, share = V((n, per, 128), F32), V((group, per, 128), F32)
    result = pl.pallas_call(
        functools.partial(kernel, n, scale, chunk),
        out_shape=(
            pltpu.VMEM((128, 128), F32),
            pltpu.VMEM((group * per, 128), F32),
        ),
        in_specs=[hbm] * 7,
        out_specs=(vmem,) * 2,
        scratch_shapes=[
            V((128, 128), BF16), V((VES, dest.shape[0]), jnp.int32), V((36, 64), BF16), V((1, 64), F32),
            V((64, 64), BF16), V((1, 64), F32), V((36, 64), BF16),
            V((256, 128), BF16), V((128, 128), BF16), V((256, 128), BF16),
            V((group * per, 128), F32), share, share, V((1, per, 128), F32), every,
            V((16 * n, 128), BF16), V((128, 16 * n), BF16), V((16 * n, 256), BF16),
            V((3, 128, 128), BF16), V((2, 128, 128), BF16), V((48, 384), BF16),
            V((128, 144), BF16), V((128, 128), BF16), V((48, 512), BF16), V((48, 768), BF16),
            V((FIELD, width), BF16), V((FIELD, width), BF16), V((n, 16, 128), BF16),
            V((2, 128, width), BF16), V((2, 128, width), BF16),
            V((2, 128, width), F32), V((2, 128, width), F32),
            V((256, 128), F32), V((256, 128), F32), V((128, 256), F32),
            pltpu.SemaphoreType.DMA((7,)),
            pltpu.SemaphoreType.DMA((4,)), pltpu.SemaphoreType.DMA((4,)),
            pltpu.SemaphoreType.DMA((2,)), pltpu.SemaphoreType.DMA((2,)),
            pltpu.SemaphoreType.REGULAR,
        ],
        compiler_params=pltpu.CompilerParams(
            collective_id=0, has_side_effects=True, vmem_limit_bytes=63 << 20
        ),
        name="deblend",
    )(
        records.reshape(128, 128), dest.T, w_in.T, b_in.reshape(1, 64), w_mid, b_mid.reshape(1, 64), w_out.T
    )
    residual, dwi, dbi, dwm, dbm, dwo = pl.pallas_call(
        deal,
        out_shape=(
            jax.ShapeDtypeStruct((128, 128), F32),
            jax.ShapeDtypeStruct((36, 64), F32),
            jax.ShapeDtypeStruct((1, 64), F32),
            jax.ShapeDtypeStruct((64, 64), F32),
            jax.ShapeDtypeStruct((1, 64), F32),
            jax.ShapeDtypeStruct((36, 64), F32),
        ),
        in_specs=[vmem] * 2,
        out_specs=(vmem,) * 6,
        name="deal",
    )(*[pltpu.with_memory_space_constraint(x, pltpu.VMEM) for x in result])
    return (
        residual.reshape(records.shape),
        dwi.T,
        dbi.reshape(64),
        dwm,
        dbm.reshape(64),
        dwo.T,
    )


def solution(mesh):
    return jax.shard_map(
        functools.partial(local, mesh.shape["rec"]),
        mesh=mesh,
        in_specs=(
            P(None, ("groups", "rec"), None, None),
            P("groups", None),
            P(),
            P(),
            P(),
            P(),
            P(),
        ),
        out_specs=(
            P(None, ("groups", "rec"), None, None),
            P("groups", None),
            P("groups"),
            P("groups", None),
            P("groups"),
            P("groups", None),
        ),
        check_vma=False,
    )
```

```python
import functools
import math

import jax
import jax.numpy as jnp
from jax import lax
from jax.experimental import pallas as pl
from jax.experimental.pallas import tpu as pltpu
from jax.sharding import PartitionSpec as P

VES = 4
F32 = jnp.float32
BF16 = jnp.bfloat16
NT = (((1,), (1,)), ((), ()))
TN = (((0,), (0,)), ((), ()))
MESH = pl.DeviceIdType.MESH

OWN, FIELD = 64, 112
GROUPS = ((1, 2), (0, 3), (-1, 4))


def iota(shape, dim):
    return lax.broadcasted_iota(jnp.int32, shape, dim)


def dot(a, b, dims=None):
    if dims is None:
        return jnp.dot(a, b, preferred_element_type=F32)
    return lax.dot_general(a, b, dims, preferred_element_type=F32)


def onehot(mask, value=1.0):
    return jnp.where(mask, value, 0.0).astype(F32)


def tap_of(k, q, flip):
    inner = k & 63
    col, trace, comp = inner >> 4, (inner >> 2) & 3, inner & 3
    at = jnp.where(k < OWN, trace, jnp.where(trace < 2, trace - 2, trace + 2))
    row = at - q + 1
    ok = (row >= 0) & (row <= 2) & (col <= 2) & (k < FIELD)
    if flip:
        row, col = 2 - row, 2 - col
    return jnp.where(ok, 9 * comp + 3 * row + col, -1)


def split3(x):
    high = x.astype(BF16)
    rest = x - high.astype(F32)
    middle = rest.astype(BF16)
    low = (rest - middle.astype(F32)).astype(BF16)
    return high, middle, low


def kernel(
    n, scale, chunk,
    rec_hbm, dest_hbm, w_in_hbm, b_in_hbm, w_mid_hbm, b_mid_hbm, w_out_hbm,
    res_ref, grad_ref,
    rec_ref, dest_ref, w_in_ref, b_in_ref, w_mid_ref, b_mid_ref, w_out_ref,
    halo, mine, qhalo, acc, packed, parts, in4, part, in5,
    sel, sel_t, sel_h, sel_q, w1, w2, w3, wm, wm_t, fold1, fold2,
    xs, qs, est, a1s, a2s, d1s, d2s, g1, g2, gm,
    load_sem, near_send, near_recv, send_sem, recv_sem, entered,
):
    me = lax.axis_index("rec")
    blocks = rec_ref.shape[0] // 8
    low, high = me > 0, me < n - 1
    group = n // 2
    plane = 8
    planes = n // plane

    barrier = pltpu.get_barrier_semaphore()
    here = (me // plane) * plane
    place = me - here

    def greet(sem, peer):
        pl.semaphore_signal(sem, inc=1, device_id={"rec": peer}, device_id_type=MESH)

    up_out = high & (place == plane - 1)
    down_out = low & (place == 0)

    @pl.when(up_out)
    def _():
        greet(barrier, me + 1)

    @pl.when(down_out)
    def _():
        greet(barrier, me - 1)

    for d in range(1, plane):
        greet(barrier, here + (place + d) % plane)
    for d in range(1, planes):
        greet(barrier, (me + d * plane) % n)

    loads = [
        pltpu.make_async_copy(src, dst, load_sem.at[i])
        for i, (src, dst) in enumerate(
            (
                (dest_hbm, dest_ref), (rec_hbm, rec_ref), (w_in_hbm, w_in_ref), (b_in_hbm, b_in_ref),
                (w_mid_hbm, w_mid_ref), (b_mid_hbm, b_mid_ref), (w_out_hbm, w_out_ref),
            )
        )
    ]
    for load in loads:
        load.start()

    def to_neighbour(src, dst, phase, up):
        return pltpu.make_async_remote_copy(
            src_ref=src.at[pl.ds(64 * up, 64)] if phase else src,
            dst_ref=dst.at[pl.ds(0 if up else dst.shape[0] // 2, dst.shape[0] // 2)],
            send_sem=near_send.at[2 * phase + up],
            recv_sem=near_recv.at[2 * phase + up],
            device_id={"rec": me + 1 if up else me - 1},
            device_id_type=MESH,
        )

    def swap(src, dst, phase):
        @pl.when(high)
        def _():
            to_neighbour(src, dst, phase, 1).start()

        @pl.when(low)
        def _():
            to_neighbour(src, dst, phase, 0).start()

    def swapped(src, dst, phase):
        @pl.when(low)
        def _():
            to_neighbour(src, dst, phase, 1).wait_recv()

        @pl.when(high)
        def _():
            to_neighbour(src, dst, phase, 0).wait_recv()

    def swap_sent(src, dst, phase):
        @pl.when(high)
        def _():
            to_neighbour(src, dst, phase, 1).wait_send()

        @pl.when(low)
        def _():
            to_neighbour(src, dst, phase, 0).wait_send()

    @pl.when(me == 0)
    def _():
        halo[0:128] = jnp.zeros((128, 128), BF16)
        qhalo[0:64] = jnp.zeros((64, 128), BF16)

    @pl.when(me == n - 1)
    def _():
        halo[128:256] = jnp.zeros((128, 128), BF16)
        qhalo[64:128] = jnp.zeros((64, 128), BF16)

    block = iota((blocks, 128), 0)
    length = dest_ref.shape[1]
    lane = iota((1, 128), 1)
    inner = (lane & 1) * 4 + (lane >> 5)
    rows = iota((16 * n, 128), 0)

    loads[0].wait()

    def targets(source, item):
        wanted = iota((blocks, length), 1) - iota((blocks, length), 0) == source * blocks
        dests = [
            jnp.broadcast_to(
                jnp.sum(jnp.where(wanted, dest_ref[v : v + 1], 0), axis=1, keepdims=True), (blocks, 128)
            )
            for v in range(VES)
        ]
        found = []
        for v in range(VES):
            own = jnp.sum(jnp.where(block == item, dests[v], 0), axis=0, keepdims=True)
            rank = jnp.zeros((blocks, 128), jnp.int32)
            for u in range(VES):
                before = (block <= item) if u < v else (block < item)
                rank = rank + jnp.where(before & (dests[u] == own), 1, 0)
            found.append((own, jnp.sum(rank, axis=0, keepdims=True)))
        return found

    def matches(targets_):
        mask = None
        for target in targets_:
            hit = rows == target
            mask = hit if mask is None else mask | hit
        return onehot(mask)

    item = (iota((blocks, 128), 1) >> 1) % blocks
    picked = matches([own * 16 + rank * 8 + inner for own, rank in targets(me, item)])
    sel[...] = picked.astype(BF16)
    sel_t[...] = picked.T.astype(BF16)
    before = [
        jnp.where((rank == 1) & low, own * 16 + inner, -1) for own, rank in targets(me - 1, item)
    ]
    after = [
        jnp.where((rank == 0) & high, own * 16 + 8 + inner, -1) for own, rank in targets(me + 1, item)
    ]
    sel_h[:, 0:128] = matches(before).astype(BF16)
    sel_h[:, 128:256] = matches(after).astype(BF16)
    item = iota((blocks, 128), 1) % blocks
    comp = (lane // blocks) & 3
    first = [
        jnp.where((rank == 1) & low & (lane < 64), own * 16 + 4 + comp, -1)
        for own, rank in targets(me - 1, item)
    ]
    second = [
        jnp.where((rank == 0) & high & (lane >= 64), own * 16 + 8 + comp, -1)
        for own, rank in targets(me + 1, item)
    ]
    sel_q[...] = matches(first + second).astype(BF16)

    loads[1].wait()
    pl.semaphore_wait(
        barrier, plane + planes - 2 + jnp.where(up_out, 1, 0) + jnp.where(down_out, 1, 0)
    )
    swap(rec_ref, halo, 0)
    for d in range(1, planes):
        greet(entered, (me + d * plane) % n)
    for load in loads[2:]:
        load.wait()

    u = iota((36, 128), 0)
    k = iota((36, 128), 1)
    bias_at = iota((128, 128), 1) - 48
    near = (iota((128, 64), 0) & 63) == iota((128, 64), 1)

    def bias_of(b_ref, at, base):
        values = jnp.sum(jnp.where(near, 0.5 * b_ref[...], 0.0), axis=1, keepdims=True)
        out = base
        for i, piece in enumerate(split3(values)):
            out = out + jnp.where(at == i, piece.astype(F32), 0.0)
        return out

    for g, qs_ in enumerate(GROUPS):
        pair = jnp.concatenate(
            [dot(w_in_ref[...], onehot(u == tap_of(k, q, False), 0.5).astype(BF16), TN) for q in qs_], axis=0
        )
        w1[g] = bias_of(b_in_ref, bias_at, pair).astype(BF16)
        w3[:, 128 * g : 128 * g + 128] = jnp.concatenate(
            [
                dot(onehot(u[:, 0:48] == tap_of(k[:, 0:48], q, True)).astype(BF16), w_out_ref[...], TN)
                for q in qs_
            ],
            axis=1,
        ).astype(BF16)
        if g < 2:
            w2[g] = jnp.concatenate(
                [dot(w_out_ref[...], onehot(u == tap_of(k, q, True), 0.5).astype(BF16), TN) for q in qs_], axis=0
            ).astype(BF16)
    outer = iota((48, 128), 1)
    inside_ = ((outer >= 64) | low) & ((outer < 64) | high)
    w3[:, 256:384] = jnp.where(inside_, w3[:, 256:384].astype(F32), 0.0).astype(BF16)
    wide = onehot((iota((64, 128), 1) & 63) == iota((64, 128), 0), 0.5).astype(BF16)
    half = dot(w_mid_ref[...], wide)
    diagonal = iota((128, 128), 0) >> 6 == iota((128, 128), 1) >> 6
    once = jnp.where(diagonal, jnp.concatenate([half, half], axis=0), 0.0)
    wm[:, 0:128] = once.astype(BF16)
    wm[:, 128:144] = bias_of(b_mid_ref, iota((128, 16), 1), jnp.zeros((128, 16), F32)).astype(BF16)
    wm_t[...] = once.T.astype(BF16)

    sample = iota((128, 128), 1)

    def taps(x):
        x = x.astype(F32)
        left = jnp.where(sample > 0, pltpu.roll(x, 1, 1), 0.0)
        right = jnp.where(sample < 127, pltpu.roll(x, 127, 1), 0.0)
        return jnp.concatenate([left.astype(BF16), x.astype(BF16), right.astype(BF16)], axis=1)

    def spread(choose, source, field, start):
        def step(c, _):
            tiles = dot(choose[pl.ds(pl.multiple_of(c * 128, 128), 128)], source).astype(BF16)
            for t in range(8):
                at = pl.ds(pl.multiple_of((c * 8 + t) * 128, 128), 128)
                for j in range(3):
                    field[start + 16 * j : start + 16 * j + 16, at] = tiles[
                        16 * t : 16 * t + 16, 128 * j : 128 * j + 128
                    ]
            return 0

        lax.fori_loop(0, n // 8, step, 0, unroll=4)

    spread(sel, taps(rec_ref[...]), xs, 0)
    ones = onehot(iota((16, n * 128), 0) < 3).astype(BF16)
    xs[48:64] = ones
    qs[48:64] = jnp.zeros((16, n * 128), BF16)

    size = chunk * 128
    ahead = chunk == n

    def columns(c):
        return pl.ds(0, size) if ahead else pl.ds(pl.multiple_of(c * size, 128), size)

    def loop(body):
        if ahead:
            body(0, 0)
        else:
            lax.fori_loop(0, n // chunk, body, 0)

    const = onehot(iota((16, size), 0) < 3).astype(BF16)

    def activate(h):
        up = 1.0 + jnp.tanh(h)
        return up, h * up

    def slope(up, a):
        return up + a * (2.0 - up)

    def first_layer(g, depth, at):
        return dot(w1[g, :, 0:depth], xs[0:depth, at])

    def mid_layer(a1):
        return dot(wm[...], jnp.concatenate([a1, const], axis=0))

    def inside(c, _):
        at = columns(c)
        up, a = activate(first_layer(0, OWN, at))
        a1 = a.astype(BF16)
        a1s[0, :, at] = a1
        h = mid_layer(a1)
        d1s[0, :, at] = slope(up, a)
        up, a = activate(h)
        a2 = a.astype(BF16)
        a2s[0, :, at] = a2
        if ahead:
            acc[:, at] = dot(w3[:, 0:128], a2)
        d2s[0, :, at] = slope(up, a)
        return 0

    loop(inside)
    for g in (g1, g2, gm):
        g[...] = jnp.zeros_like(g)
    u = iota((48, 128), 0)
    k = iota((48, 128), 1)
    for i, q in enumerate(GROUPS[0] + GROUPS[1]):
        at = slice(128 * i, 128 * i + 128)
        fold1[:, at] = onehot((u == tap_of(k, q, False)) | ((k == 48) & (u == 36))).astype(BF16)
        fold2[:, at] = onehot(u == tap_of(k, q, True)).astype(BF16)
    for i in range(2):
        fold2[:, 512 + 128 * i : 640 + 128 * i] = onehot((k == 0) & (u == 36)).astype(BF16)

    swapped(rec_ref, halo, 0)
    spread(sel_h, jnp.concatenate([taps(halo[0:128]), taps(halo[128:256])], axis=0), xs, OWN)

    small = iota((16, 128), 1)

    def border(c, _):
        at = columns(c)
        h1 = first_layer(1, FIELD, at)
        x1 = first_layer(2, FIELD, at)
        d1s[1, :, at] = h1
        a1 = activate(h1)[1].astype(BF16)
        a1s[1, :, at] = a1
        h2 = mid_layer(a1)
        x2 = mid_layer(activate(x1)[1].astype(BF16))
        d2s[1, :, at] = h2
        a2 = activate(h2)[1].astype(BF16)
        a2s[1, :, at] = a2
        terms = acc[:, at] if ahead else dot(w3[:, 0:128], a2s[0, :, at])
        terms = terms + dot(w3[:, 128:256], a2)
        terms = terms + dot(w3[:, 256:384], activate(x2)[1].astype(BF16))
        for t in range(chunk):
            x = terms[:, 128 * t : 128 * t + 128]
            first = jnp.where(small < 127, pltpu.roll(x[0:16], 127, 1), 0.0)
            last = jnp.where(small > 0, pltpu.roll(x[32:48], 1, 1), 0.0)
            est[c * chunk + t] = (x[16:32] + first + last).astype(BF16)
        return 0

    loop(border)

    residual = dot(sel_t[...], est[...].reshape(16 * n, 128)) - rec_ref[...].astype(F32)
    res_ref[...] = residual
    mine[0:64] = res_ref[pl.ds(0, 64, stride=2)].astype(BF16)
    mine[64:128] = res_ref[pl.ds(1, 64, stride=2)].astype(BF16)
    swap(mine, qhalo, 1)
    spread(sel, taps(residual.astype(BF16)), qs, 0)
    def backward(g, depth):
        def step(c, _):
            at = columns(c)
            row = slice(128 * g, 128 * g + 128)
            field = qs[0:depth, at]
            da2 = dot(w2[g, :, 0:depth], field)
            g2[row, 0:depth] += dot(a2s[g, :, at], field, NT)
            dz2 = (da2 * d2s[g, :, at]).astype(BF16)
            da1 = dot(wm_t[...], dz2)
            gm[:, 0:144] += dot(dz2, jnp.concatenate([a1s[g, :, at], const], axis=0), NT)
            dz1 = (da1 * d1s[g, :, at]).astype(BF16)
            g1[row, 0:depth] += dot(dz1, xs[0:depth, at], NT)
            return 0

        loop(step)

    def slopes(c, _):
        at = columns(c)
        for d in (d1s, d2s):
            d[1, :, at] = slope(*activate(d[1, :, at]))
        return 0

    backward(0, OWN)
    loop(slopes)
    swapped(mine, qhalo, 1)
    spread(sel_q, taps(qhalo[...]), qs, OWN)
    backward(1, FIELD)

    def folded(fold, pieces):
        total = None
        for piece in split3(jnp.concatenate(pieces, axis=1)):
            term = dot(fold[...], piece, NT)
            total = term if total is None else total + term
        return total

    four = [slice(64 * i, 64 * i + 64) for i in range(4)]
    second = folded(fold2, [g2[at] for at in four] + [gm[0:64, 128:256], gm[64:128, 128:256]])
    first = folded(fold1, [g1[at] for at in four])
    packed[0:40] = jnp.concatenate([first[0:40], second[0:40]], axis=1)
    square = gm[0:64, 0:128] + pltpu.roll(gm[64:128, 0:128], 64, 1)
    packed[40:72] = jnp.where(iota((32, 128), 1) < 64, square[0:32], pltpu.roll(square[32:64], 64, 1))
    packed[72:] = jnp.zeros((packed.shape[0] - 72, 128), F32)
    per = parts.shape[1]
    for i in range(group):
        parts[i] = packed[per * i : per * i + per]

    def send(src, dst, phase, peer):
        pltpu.make_async_remote_copy(
            src_ref=src,
            dst_ref=dst,
            send_sem=send_sem.at[phase],
            recv_sem=recv_sem.at[phase],
            device_id={"rec": peer},
            device_id_type=MESH,
        ).start()

    def wait(ref, count, sem):
        every = ref.at[pl.ds(0, count)]
        pltpu.make_async_copy(every, every, sem).wait()

    base = (me // group) * group
    index = me - base
    pl.semaphore_wait(entered, planes - 1)
    for d in range(group - 1, 0, -1):
        to = index ^ d
        send(parts.at[to], in4.at[index], 0, base + to)
    in4[index] = parts[index]
    wait(in4, group - 1, recv_sem.at[0])
    part[...] = jnp.sum(in4[...], axis=0, keepdims=True) * scale
    for d in range(n - 1, 0, -1):
        send(part.at[0], in5.at[me], 1, me ^ d)
    in5[me] = part[0]
    wait(in5, n - 1, recv_sem.at[1])
    for i in range(group):
        grad_ref[per * i : per * i + per] = in5[i] + in5[i + group]
    swap_sent(rec_ref, halo, 0)
    swap_sent(mine, qhalo, 1)
    wait(parts, group - 1, send_sem.at[0])
    wait(in5, n - 1, send_sem.at[1])


def deal(res_ref, grad_ref, out_ref, dwi_ref, dbi_ref, dwm_ref, dbm_ref, dwo_ref):
    out_ref[...] = res_ref[...]
    dwi_ref[...] = grad_ref[0:36, 0:64]
    dbi_ref[...] = grad_ref[36:37, 0:64]
    dwm_ref[0:32] = grad_ref[40:72, 0:64]
    dwo_ref[...] = pltpu.roll(grad_ref[0:40], 64, 1)[0:36, 0:64]
    dbm_ref[...] = pltpu.roll(grad_ref[0:40], 64, 1)[36:37, 0:64]
    dwm_ref[32:64] = pltpu.roll(grad_ref[40:72], 64, 1)[:, 0:64]


def local(n, records, dest, w_in, b_in, w_mid, b_mid, w_out):
    parts, blocks, traces, samples = records.shape
    width = n * samples
    group = n // 2
    per = -(-72 // group)
    chunk = n if n <= 32 else 4
    scale = 1.0 / math.sqrt(parts * blocks * n * traces * samples)
    vmem = pl.BlockSpec(memory_space=pltpu.VMEM)
    V = pltpu.VMEM
    hbm = pl.BlockSpec(memory_space=pl.ANY)
    every, share = V((n, per, 128), F32), V((group, per, 128), F32)
    result = pl.pallas_call(
        functools.partial(kernel, n, scale, chunk),
        out_shape=(
            pltpu.VMEM((128, 128), F32),
            pltpu.VMEM((group * per, 128), F32),
        ),
        in_specs=[hbm] * 7,
        out_specs=(vmem,) * 2,
        scratch_shapes=[
            V((128, 128), BF16), V((VES, dest.shape[0]), jnp.int32), V((36, 64), BF16), V((1, 64), F32),
            V((64, 64), BF16), V((1, 64), F32), V((36, 64), BF16),
            V((256, 128), BF16), V((128, 128), BF16), V((128, 128), BF16), V((48, width if chunk == n else 128), F32),
            V((group * per, 128), F32), share, share, V((1, per, 128), F32), every,
            V((16 * n, 128), BF16), V((128, 16 * n), BF16), V((16 * n, 256), BF16),
            V((16 * n, 128), BF16),
            V((3, 128, 128), BF16), V((2, 128, 128), BF16), V((48, 384), BF16),
            V((128, 144), BF16), V((128, 128), BF16), V((48, 512), BF16), V((48, 768), BF16),
            V((FIELD, width), BF16), V((FIELD, width), BF16), V((n, 16, 128), BF16),
            V((2, 128, width), BF16), V((2, 128, width), BF16),
            V((2, 128, width), F32), V((2, 128, width), F32),
            V((256, 128), F32), V((256, 128), F32), V((128, 256), F32),
            pltpu.SemaphoreType.DMA((7,)),
            pltpu.SemaphoreType.DMA((4,)), pltpu.SemaphoreType.DMA((4,)),
            pltpu.SemaphoreType.DMA((2,)), pltpu.SemaphoreType.DMA((2,)),
            pltpu.SemaphoreType.REGULAR,
        ],
        compiler_params=pltpu.CompilerParams(
            collective_id=0, has_side_effects=True, vmem_limit_bytes=63 << 20
        ),
        name="deblend",
    )(
        records.reshape(128, 128), dest.T, w_in.T, b_in.reshape(1, 64), w_mid, b_mid.reshape(1, 64), w_out.T
    )
    residual, dwi, dbi, dwm, dbm, dwo = pl.pallas_call(
        deal,
        out_shape=(
            jax.ShapeDtypeStruct((128, 128), F32),
            jax.ShapeDtypeStruct((36, 64), F32),
            jax.ShapeDtypeStruct((1, 64), F32),
            jax.ShapeDtypeStruct((64, 64), F32),
            jax.ShapeDtypeStruct((1, 64), F32),
            jax.ShapeDtypeStruct((36, 64), F32),
        ),
        in_specs=[vmem] * 2,
        out_specs=(vmem,) * 6,
        name="deal",
    )(*[pltpu.with_memory_space_constraint(x, pltpu.VMEM) for x in result])
    return (
        residual.reshape(records.shape),
        dwi.T,
        dbi.reshape(64),
        dwm,
        dbm.reshape(64),
        dwo.T,
    )


def solution(mesh):
    return jax.shard_map(
        functools.partial(local, mesh.shape["rec"]),
        mesh=mesh,
        in_specs=(
            P(None, ("groups", "rec"), None, None),
            P("groups", None),
            P(),
            P(),
            P(),
            P(),
            P(),
        ),
        out_specs=(
            P(None, ("groups", "rec"), None, None),
            P("groups", None),
            P("groups"),
            P("groups", None),
            P("groups"),
            P("groups", None),
        ),
        check_vma=False,
    )
```

```python
import functools
import math

import jax
import jax.numpy as jnp
from jax import lax
from jax.experimental import pallas as pl
from jax.experimental.pallas import tpu as pltpu
from jax.sharding import PartitionSpec as P

VES = 4
F32 = jnp.float32
BF16 = jnp.bfloat16
NT = (((1,), (1,)), ((), ()))
TN = (((0,), (0,)), ((), ()))
MESH = pl.DeviceIdType.MESH

OWN, FIELD = 64, 112
GROUPS = ((1, 2), (0, 3), (-1, 4))


def iota(shape, dim):
    return lax.broadcasted_iota(jnp.int32, shape, dim)


def dot(a, b, dims=None):
    if dims is None:
        return jnp.dot(a, b, preferred_element_type=F32)
    return lax.dot_general(a, b, dims, preferred_element_type=F32)


def onehot(mask, value=1.0):
    return jnp.where(mask, value, 0.0).astype(F32)


def tap_of(k, q, flip):
    inner = k & 63
    col, trace, comp = inner >> 4, (inner >> 2) & 3, inner & 3
    at = jnp.where(k < OWN, trace, jnp.where(trace < 2, trace - 2, trace + 2))
    row = at - q + 1
    ok = (row >= 0) & (row <= 2) & (col <= 2) & (k < FIELD)
    if flip:
        row, col = 2 - row, 2 - col
    return jnp.where(ok, 9 * comp + 3 * row + col, -1)


def split3(x):
    high = x.astype(BF16)
    rest = x - high.astype(F32)
    middle = rest.astype(BF16)
    low = (rest - middle.astype(F32)).astype(BF16)
    return high, middle, low


def kernel(
    n, scale, chunk,
    rec_hbm, dest_hbm, w_in_hbm, b_in_hbm, w_mid_hbm, b_mid_hbm, w_out_hbm,
    res_ref, grad_ref,
    rec_ref, dest_ref, w_in_ref, b_in_ref, w_mid_ref, b_mid_ref, w_out_ref,
    halo, mine, qhalo, acc, packed, parts, in4, part, in5,
    sel, sel_t, sel_h, sel_q, w1, w2, w3, wm, wm_t, fold1, fold2,
    xs, qs, est, a1s, a2s, d1s, d2s, g1, g2, gm,
    load_sem, near_send, near_recv, send_sem, recv_sem, entered,
):
    me = lax.axis_index("rec")
    blocks = rec_ref.shape[0] // 8
    low, high = me > 0, me < n - 1
    group = n // 2
    plane = 8
    steps = [plane << i for i in range((n // plane).bit_length() - 1)]

    barrier = pltpu.get_barrier_semaphore()
    here = (me // plane) * plane
    place = me - here

    def greet(sem, peer):
        pl.semaphore_signal(sem, inc=1, device_id={"rec": peer}, device_id_type=MESH)

    up_out = high & (place == plane - 1)
    down_out = low & (place == 0)

    @pl.when(up_out)
    def _():
        greet(barrier, me + 1)

    @pl.when(down_out)
    def _():
        greet(barrier, me - 1)

    for d in range(1, plane):
        greet(barrier, here + (place + d) % plane)
    for step in steps:
        greet(barrier, me ^ step)

    loads = [
        pltpu.make_async_copy(src, dst, load_sem.at[i])
        for i, (src, dst) in enumerate(
            (
                (dest_hbm, dest_ref), (rec_hbm, rec_ref), (w_in_hbm, w_in_ref), (b_in_hbm, b_in_ref),
                (w_mid_hbm, w_mid_ref), (b_mid_hbm, b_mid_ref), (w_out_hbm, w_out_ref),
            )
        )
    ]
    for load in loads:
        load.start()

    def to_neighbour(src, dst, phase, up):
        return pltpu.make_async_remote_copy(
            src_ref=src.at[pl.ds(64 * up, 64)] if phase else src,
            dst_ref=dst.at[pl.ds(0 if up else dst.shape[0] // 2, dst.shape[0] // 2)],
            send_sem=near_send.at[2 * phase + up],
            recv_sem=near_recv.at[2 * phase + up],
            device_id={"rec": me + 1 if up else me - 1},
            device_id_type=MESH,
        )

    def swap(src, dst, phase):
        @pl.when(high)
        def _():
            to_neighbour(src, dst, phase, 1).start()

        @pl.when(low)
        def _():
            to_neighbour(src, dst, phase, 0).start()

    def swapped(src, dst, phase):
        @pl.when(low)
        def _():
            to_neighbour(src, dst, phase, 1).wait_recv()

        @pl.when(high)
        def _():
            to_neighbour(src, dst, phase, 0).wait_recv()

    def swap_sent(src, dst, phase):
        @pl.when(high)
        def _():
            to_neighbour(src, dst, phase, 1).wait_send()

        @pl.when(low)
        def _():
            to_neighbour(src, dst, phase, 0).wait_send()

    @pl.when(me == 0)
    def _():
        halo[0:128] = jnp.zeros((128, 128), BF16)
        qhalo[0:64] = jnp.zeros((64, 128), BF16)

    @pl.when(me == n - 1)
    def _():
        halo[128:256] = jnp.zeros((128, 128), BF16)
        qhalo[64:128] = jnp.zeros((64, 128), BF16)

    block = iota((blocks, 128), 0)
    length = dest_ref.shape[1]
    lane = iota((1, 128), 1)
    inner = (lane & 1) * 4 + (lane >> 5)
    rows = iota((16 * n, 128), 0)

    for g in (g1, g2, gm):
        g[...] = jnp.zeros_like(g)
    u = iota((48, 128), 0)
    k = iota((48, 128), 1)
    for i, q in enumerate(GROUPS[0] + GROUPS[1]):
        at = slice(128 * i, 128 * i + 128)
        fold1[:, at] = onehot((u == tap_of(k, q, False)) | ((k == 48) & (u == 36))).astype(BF16)
        fold2[:, at] = onehot(u == tap_of(k, q, True)).astype(BF16)
    for i in range(2):
        fold2[:, 512 + 128 * i : 640 + 128 * i] = onehot((k == 0) & (u == 36)).astype(BF16)

    ones = onehot(iota((16, n * 128), 0) < 3).astype(BF16)
    xs[48:64] = ones
    qs[48:64] = jnp.zeros((16, n * 128), BF16)
    loads[0].wait()

    def targets(source, item):
        wanted = iota((blocks, length), 1) - iota((blocks, length), 0) == source * blocks
        dests = [
            jnp.broadcast_to(
                jnp.sum(jnp.where(wanted, dest_ref[v : v + 1], 0), axis=1, keepdims=True), (blocks, 128)
            )
            for v in range(VES)
        ]
        found = []
        for v in range(VES):
            own = jnp.sum(jnp.where(block == item, dests[v], 0), axis=0, keepdims=True)
            rank = jnp.zeros((blocks, 128), jnp.int32)
            for u in range(VES):
                before = (block <= item) if u < v else (block < item)
                rank = rank + jnp.where(before & (dests[u] == own), 1, 0)
            found.append((own, jnp.sum(rank, axis=0, keepdims=True)))
        return found

    def matches(targets_):
        mask = None
        for target in targets_:
            hit = rows == target
            mask = hit if mask is None else mask | hit
        return onehot(mask)

    item = (iota((blocks, 128), 1) >> 1) % blocks
    picked = matches([own * 16 + rank * 8 + inner for own, rank in targets(me, item)])
    sel[...] = picked.astype(BF16)
    sel_t[...] = picked.T.astype(BF16)
    before = [
        jnp.where((rank == 1) & low, own * 16 + inner, -1) for own, rank in targets(me - 1, item)
    ]
    after = [
        jnp.where((rank == 0) & high, own * 16 + 8 + inner, -1) for own, rank in targets(me + 1, item)
    ]
    sel_h[:, 0:128] = matches(before).astype(BF16)
    sel_h[:, 128:256] = matches(after).astype(BF16)
    loads[1].wait()
    pl.semaphore_wait(
        barrier, plane - 1 + len(steps) + jnp.where(up_out, 1, 0) + jnp.where(down_out, 1, 0)
    )
    swap(rec_ref, halo, 0)
    greet(entered.at[0], me ^ steps[0])
    item = iota((blocks, 128), 1) % blocks
    comp = (lane // blocks) & 3
    first = [
        jnp.where((rank == 1) & low & (lane < 64), own * 16 + 4 + comp, -1)
        for own, rank in targets(me - 1, item)
    ]
    second = [
        jnp.where((rank == 0) & high & (lane >= 64), own * 16 + 8 + comp, -1)
        for own, rank in targets(me + 1, item)
    ]
    sel_q[...] = matches(first + second).astype(BF16)

    for load in loads[2:]:
        load.wait()

    u = iota((36, 128), 0)
    k = iota((36, 128), 1)
    bias_at = iota((128, 128), 1) - 48
    near = (iota((128, 64), 0) & 63) == iota((128, 64), 1)

    def bias_of(b_ref, at, base):
        values = jnp.sum(jnp.where(near, 0.5 * b_ref[...], 0.0), axis=1, keepdims=True)
        out = base
        for i, piece in enumerate(split3(values)):
            out = out + jnp.where(at == i, piece.astype(F32), 0.0)
        return out

    for g, qs_ in enumerate(GROUPS):
        pair = jnp.concatenate(
            [dot(w_in_ref[...], onehot(u == tap_of(k, q, False), 0.5).astype(BF16), TN) for q in qs_], axis=0
        )
        w1[g] = bias_of(b_in_ref, bias_at, pair).astype(BF16)
        w3[:, 128 * g : 128 * g + 128] = jnp.concatenate(
            [
                dot(onehot(u[:, 0:48] == tap_of(k[:, 0:48], q, True)).astype(BF16), w_out_ref[...], TN)
                for q in qs_
            ],
            axis=1,
        ).astype(BF16)
        if g < 2:
            w2[g] = jnp.concatenate(
                [dot(w_out_ref[...], onehot(u == tap_of(k, q, True), 0.5).astype(BF16), TN) for q in qs_], axis=0
            ).astype(BF16)
    outer = iota((48, 128), 1)
    inside_ = ((outer >= 64) | low) & ((outer < 64) | high)
    w3[:, 256:384] = jnp.where(inside_, w3[:, 256:384].astype(F32), 0.0).astype(BF16)
    wide = onehot((iota((64, 128), 1) & 63) == iota((64, 128), 0), 0.5).astype(BF16)
    half = dot(w_mid_ref[...], wide)
    diagonal = iota((128, 128), 0) >> 6 == iota((128, 128), 1) >> 6
    once = jnp.where(diagonal, jnp.concatenate([half, half], axis=0), 0.0)
    wm[:, 0:128] = once.astype(BF16)
    wm[:, 128:144] = bias_of(b_mid_ref, iota((128, 16), 1), jnp.zeros((128, 16), F32)).astype(BF16)
    wm_t[...] = once.T.astype(BF16)

    sample = iota((128, 128), 1)

    def taps(x):
        x = x.astype(F32)
        left = jnp.where(sample > 0, pltpu.roll(x, 1, 1), 0.0)
        right = jnp.where(sample < 127, pltpu.roll(x, 127, 1), 0.0)
        return jnp.concatenate([left.astype(BF16), x.astype(BF16), right.astype(BF16)], axis=1)

    def spread(choose, source, field, start):
        def step(c, _):
            tiles = dot(choose[pl.ds(pl.multiple_of(c * 128, 128), 128)], source).astype(BF16)
            for t in range(8):
                at = pl.ds(pl.multiple_of((c * 8 + t) * 128, 128), 128)
                for j in range(3):
                    field[start + 16 * j : start + 16 * j + 16, at] = tiles[
                        16 * t : 16 * t + 16, 128 * j : 128 * j + 128
                    ]
            return 0

        lax.fori_loop(0, n // 8, step, 0, unroll=4)

    spread(sel, taps(rec_ref[...]), xs, 0)

    size = chunk * 128
    ahead = chunk == n

    def columns(c):
        return pl.ds(0, size) if ahead else pl.ds(pl.multiple_of(c * size, 128), size)

    def loop(body):
        if ahead:
            body(0, 0)
        else:
            lax.fori_loop(0, n // chunk, body, 0)

    const = onehot(iota((16, size), 0) < 3).astype(BF16)

    def activate(h):
        up = 1.0 + jnp.tanh(h)
        return up, h * up

    def slope(up, a):
        return up + a * (2.0 - up)

    def first_layer(g, depth, at):
        return dot(w1[g, :, 0:depth], xs[0:depth, at])

    def mid_layer(a1):
        return dot(wm[...], jnp.concatenate([a1, const], axis=0))

    def inside(c, _):
        at = columns(c)
        up, a = activate(first_layer(0, OWN, at))
        a1 = a.astype(BF16)
        a1s[0, :, at] = a1
        h = mid_layer(a1)
        d1s[0, :, at] = slope(up, a)
        up, a = activate(h)
        a2 = a.astype(BF16)
        a2s[0, :, at] = a2
        if ahead:
            acc[:, at] = dot(w3[:, 0:128], a2)
        d2s[0, :, at] = slope(up, a)
        return 0

    loop(inside)
    swapped(rec_ref, halo, 0)
    spread(sel_h, jnp.concatenate([taps(halo[0:128]), taps(halo[128:256])], axis=0), xs, OWN)

    small = iota((16, 128), 1)

    def border(c, _):
        at = columns(c)
        h1 = first_layer(1, FIELD, at)
        x1 = first_layer(2, FIELD, at)
        d1s[1, :, at] = h1
        a1 = activate(h1)[1].astype(BF16)
        a1s[1, :, at] = a1
        h2 = mid_layer(a1)
        x2 = mid_layer(activate(x1)[1].astype(BF16))
        d2s[1, :, at] = h2
        a2 = activate(h2)[1].astype(BF16)
        a2s[1, :, at] = a2
        terms = acc[:, at] if ahead else dot(w3[:, 0:128], a2s[0, :, at])
        terms = terms + dot(w3[:, 128:256], a2)
        terms = terms + dot(w3[:, 256:384], activate(x2)[1].astype(BF16))
        for t in range(chunk):
            x = terms[:, 128 * t : 128 * t + 128]
            first = jnp.where(small < 127, pltpu.roll(x[0:16], 127, 1), 0.0)
            last = jnp.where(small > 0, pltpu.roll(x[32:48], 1, 1), 0.0)
            est[c * chunk + t] = (x[16:32] + first + last).astype(BF16)
        return 0

    loop(border)

    residual = dot(sel_t[...], est[...].reshape(16 * n, 128)) - rec_ref[...].astype(F32)
    res_ref[...] = residual
    for i, step in enumerate(steps[1:]):
        pl.semaphore_wait(entered.at[i], 1)
        greet(entered.at[i + 1], me ^ step)
    mine[0:64] = res_ref[pl.ds(0, 64, stride=2)].astype(BF16)
    mine[64:128] = res_ref[pl.ds(1, 64, stride=2)].astype(BF16)
    swap(mine, qhalo, 1)
    spread(sel, taps(residual.astype(BF16)), qs, 0)
    def backward(g, depth):
        def step(c, _):
            at = columns(c)
            row = slice(128 * g, 128 * g + 128)
            field = qs[0:depth, at]
            da2 = dot(w2[g, :, 0:depth], field)
            g2[row, 0:depth] += dot(a2s[g, :, at], field, NT)
            dz2 = (da2 * d2s[g, :, at]).astype(BF16)
            da1 = dot(wm_t[...], dz2)
            gm[:, 0:144] += dot(dz2, jnp.concatenate([a1s[g, :, at], const], axis=0), NT)
            dz1 = (da1 * d1s[g, :, at]).astype(BF16)
            g1[row, 0:depth] += dot(dz1, xs[0:depth, at], NT)
            return 0

        loop(step)

    def slopes(c, _):
        at = columns(c)
        for d in (d1s, d2s):
            d[1, :, at] = slope(*activate(d[1, :, at]))
        return 0

    backward(0, OWN)
    loop(slopes)
    swapped(mine, qhalo, 1)
    spread(sel_q, taps(qhalo[...]), qs, OWN)
    backward(1, FIELD)

    def folded(fold, pieces):
        joined = jnp.concatenate(split3(jnp.concatenate(pieces, axis=1)), axis=0)
        term = dot(fold[...], joined, NT)
        return term[:, 0:64] + term[:, 64:128] + term[:, 128:192]

    four = [slice(64 * i, 64 * i + 64) for i in range(4)]
    second = folded(fold2, [g2[at] for at in four] + [gm[0:64, 128:256], gm[64:128, 128:256]])
    first = folded(fold1, [g1[at] for at in four])
    packed[0:40] = jnp.concatenate([first[0:40], second[0:40]], axis=1)
    square = gm[0:64, 0:128] + pltpu.roll(gm[64:128, 0:128], 64, 1)
    packed[40:72] = jnp.where(iota((32, 128), 1) < 64, square[0:32], pltpu.roll(square[32:64], 64, 1))
    packed[72:] = jnp.zeros((packed.shape[0] - 72, 128), F32)
    per = parts.shape[1]
    for i in range(group):
        parts[i] = packed[per * i : per * i + per]

    def send(src, dst, phase, peer):
        pltpu.make_async_remote_copy(
            src_ref=src,
            dst_ref=dst,
            send_sem=send_sem.at[phase],
            recv_sem=recv_sem.at[phase],
            device_id={"rec": peer},
            device_id_type=MESH,
        ).start()

    def wait(ref, count, sem):
        every = ref.at[pl.ds(0, count)]
        pltpu.make_async_copy(every, every, sem).wait()

    base = (me // group) * group
    index = me - base
    pl.semaphore_wait(entered.at[len(steps) - 1], 1)
    for d in range(group - 1, 0, -1):
        to = index ^ d
        send(parts.at[to], in4.at[index], 0, base + to)
    in4[index] = parts[index]
    wait(in4, group - 1, recv_sem.at[0])
    part[...] = jnp.sum(in4[...], axis=0, keepdims=True) * scale
    for d in range(n - 1, 0, -1):
        send(part.at[0], in5.at[me], 1, me ^ d)
    in5[me] = part[0]
    wait(in5, n - 1, recv_sem.at[1])
    for i in range(group):
        grad_ref[per * i : per * i + per] = in5[i] + in5[i + group]
    swap_sent(rec_ref, halo, 0)
    swap_sent(mine, qhalo, 1)
    wait(parts, group - 1, send_sem.at[0])
    wait(in5, n - 1, send_sem.at[1])


def deal(res_ref, grad_ref, out_ref, dwi_ref, dbi_ref, dwm_ref, dbm_ref, dwo_ref):
    out_ref[...] = res_ref[...]
    dwi_ref[...] = grad_ref[0:36, 0:64]
    dbi_ref[...] = grad_ref[36:37, 0:64]
    dwm_ref[0:32] = grad_ref[40:72, 0:64]
    dwo_ref[...] = pltpu.roll(grad_ref[0:40], 64, 1)[0:36, 0:64]
    dbm_ref[...] = pltpu.roll(grad_ref[0:40], 64, 1)[36:37, 0:64]
    dwm_ref[32:64] = pltpu.roll(grad_ref[40:72], 64, 1)[:, 0:64]


def local(n, records, dest, w_in, b_in, w_mid, b_mid, w_out):
    parts, blocks, traces, samples = records.shape
    width = n * samples
    group = n // 2
    per = -(-72 // group)
    chunk = n if n <= 32 else 4
    scale = 1.0 / math.sqrt(parts * blocks * n * traces * samples)
    vmem = pl.BlockSpec(memory_space=pltpu.VMEM)
    V = pltpu.VMEM
    hbm = pl.BlockSpec(memory_space=pl.ANY)
    every, share = V((n, per, 128), F32), V((group, per, 128), F32)
    result = pl.pallas_call(
        functools.partial(kernel, n, scale, chunk),
        out_shape=(
            pltpu.VMEM((128, 128), F32),
            pltpu.VMEM((group * per, 128), F32),
        ),
        in_specs=[hbm] * 7,
        out_specs=(vmem,) * 2,
        scratch_shapes=[
            V((128, 128), BF16), V((VES, dest.shape[0]), jnp.int32), V((36, 64), BF16), V((1, 64), F32),
            V((64, 64), BF16), V((1, 64), F32), V((36, 64), BF16),
            V((256, 128), BF16), V((128, 128), BF16), V((128, 128), BF16), V((48, width if chunk == n else 128), F32),
            V((group * per, 128), F32), share, share, V((1, per, 128), F32), every,
            V((16 * n, 128), BF16), V((128, 16 * n), BF16), V((16 * n, 256), BF16),
            V((16 * n, 128), BF16),
            V((3, 128, 128), BF16), V((2, 128, 128), BF16), V((48, 384), BF16),
            V((128, 144), BF16), V((128, 128), BF16), V((48, 512), BF16), V((48, 768), BF16),
            V((FIELD, width), BF16), V((FIELD, width), BF16), V((n, 16, 128), BF16),
            V((2, 128, width), BF16), V((2, 128, width), BF16),
            V((2, 128, width), F32), V((2, 128, width), F32),
            V((256, 128), F32), V((256, 128), F32), V((128, 256), F32),
            pltpu.SemaphoreType.DMA((7,)),
            pltpu.SemaphoreType.DMA((4,)), pltpu.SemaphoreType.DMA((4,)),
            pltpu.SemaphoreType.DMA((2,)), pltpu.SemaphoreType.DMA((2,)),
            pltpu.SemaphoreType.REGULAR(((n // 8).bit_length() - 1,)),
        ],
        compiler_params=pltpu.CompilerParams(
            collective_id=0, has_side_effects=True, vmem_limit_bytes=63 << 20
        ),
        name="deblend",
    )(
        records.reshape(128, 128), dest.T, w_in.T, b_in.reshape(1, 64), w_mid, b_mid.reshape(1, 64), w_out.T
    )
    residual, dwi, dbi, dwm, dbm, dwo = pl.pallas_call(
        deal,
        out_shape=(
            jax.ShapeDtypeStruct((128, 128), F32),
            jax.ShapeDtypeStruct((36, 64), F32),
            jax.ShapeDtypeStruct((1, 64), F32),
            jax.ShapeDtypeStruct((64, 64), F32),
            jax.ShapeDtypeStruct((1, 64), F32),
            jax.ShapeDtypeStruct((36, 64), F32),
        ),
        in_specs=[vmem] * 2,
        out_specs=(vmem,) * 6,
        name="deal",
    )(*[pltpu.with_memory_space_constraint(x, pltpu.VMEM) for x in result])
    return (
        residual.reshape(records.shape),
        dwi.T,
        dbi.reshape(64),
        dwm,
        dbm.reshape(64),
        dwo.T,
    )


def solution(mesh):
    return jax.shard_map(
        functools.partial(local, mesh.shape["rec"]),
        mesh=mesh,
        in_specs=(
            P(None, ("groups", "rec"), None, None),
            P("groups", None),
            P(),
            P(),
            P(),
            P(),
            P(),
        ),
        out_specs=(
            P(None, ("groups", "rec"), None, None),
            P("groups", None),
            P("groups"),
            P("groups", None),
            P("groups"),
            P("groups", None),
        ),
        check_vma=False,
    )
```

```python
import functools
import math

import jax
import jax.numpy as jnp
from jax import lax
from jax.experimental import pallas as pl
from jax.experimental.pallas import tpu as pltpu
from jax.sharding import PartitionSpec as P

VES = 4
F32 = jnp.float32
BF16 = jnp.bfloat16
NT = (((1,), (1,)), ((), ()))
TN = (((0,), (0,)), ((), ()))
MESH = pl.DeviceIdType.MESH

OWN, FIELD = 64, 112
GROUPS = ((1, 2), (0, 3), (-1, 4))


def iota(shape, dim):
    return lax.broadcasted_iota(jnp.int32, shape, dim)


def dot(a, b, dims=None):
    if dims is None:
        return jnp.dot(a, b, preferred_element_type=F32)
    return lax.dot_general(a, b, dims, preferred_element_type=F32)


def onehot(mask, value=1.0):
    return jnp.where(mask, value, 0.0).astype(F32)


def tap_of(k, q, flip):
    inner = k & 63
    col, trace, comp = inner >> 4, (inner >> 2) & 3, inner & 3
    at = jnp.where(k < OWN, trace, jnp.where(trace < 2, trace - 2, trace + 2))
    row = at - q + 1
    ok = (row >= 0) & (row <= 2) & (col <= 2) & (k < FIELD)
    if flip:
        row, col = 2 - row, 2 - col
    return jnp.where(ok, 9 * comp + 3 * row + col, -1)


def split3(x):
    high = x.astype(BF16)
    rest = x - high.astype(F32)
    middle = rest.astype(BF16)
    low = (rest - middle.astype(F32)).astype(BF16)
    return high, middle, low


def kernel(
    n, scale, chunk,
    rec_hbm, dest_hbm, w_in_hbm, b_in_hbm, w_mid_hbm, b_mid_hbm, w_out_hbm,
    res_ref, grad_ref,
    rec_ref, dest_ref, w_in_ref, b_in_ref, w_mid_ref, b_mid_ref, w_out_ref,
    halo, mine, qhalo, acc, packed, parts, in4, part, in5,
    sel, sel_t, sel_h, sel_q, w1, w2, w3, wm, wm_t, fold1, fold2,
    xs, qs, est, a1s, a2s, d1s, d2s, g1, g2, gm,
    load_sem, near_send, near_recv, send_sem, recv_sem, entered,
):
    me = lax.axis_index("rec")
    blocks = rec_ref.shape[0] // 8
    low, high = me > 0, me < n - 1
    group = n // 2
    plane = 8
    planes = n // plane

    barrier = pltpu.get_barrier_semaphore()
    here = (me // plane) * plane
    place = me - here

    def greet(sem, peer):
        pl.semaphore_signal(sem, inc=1, device_id={"rec": peer}, device_id_type=MESH)

    up_out = high & (place == plane - 1)
    down_out = low & (place == 0)

    @pl.when(up_out)
    def _():
        greet(barrier, me + 1)

    @pl.when(down_out)
    def _():
        greet(barrier, me - 1)

    for d in range(1, plane):
        greet(barrier, here + (place + d) % plane)
    for d in range(1, planes):
        greet(barrier, (me + d * plane) % n)

    loads = [
        pltpu.make_async_copy(src, dst, load_sem.at[i])
        for i, (src, dst) in enumerate(
            (
                (dest_hbm, dest_ref), (rec_hbm, rec_ref), (w_in_hbm, w_in_ref), (b_in_hbm, b_in_ref),
                (w_mid_hbm, w_mid_ref), (b_mid_hbm, b_mid_ref), (w_out_hbm, w_out_ref),
            )
        )
    ]
    for load in loads:
        load.start()

    def to_neighbour(src, dst, phase, up):
        return pltpu.make_async_remote_copy(
            src_ref=src.at[pl.ds(64 * up, 64)] if phase else src,
            dst_ref=dst.at[pl.ds(0 if up else dst.shape[0] // 2, dst.shape[0] // 2)],
            send_sem=near_send.at[2 * phase + up],
            recv_sem=near_recv.at[2 * phase + up],
            device_id={"rec": me + 1 if up else me - 1},
            device_id_type=MESH,
        )

    def swap(src, dst, phase):
        @pl.when(high)
        def _():
            to_neighbour(src, dst, phase, 1).start()

        @pl.when(low)
        def _():
            to_neighbour(src, dst, phase, 0).start()

    def swapped(src, dst, phase):
        @pl.when(low)
        def _():
            to_neighbour(src, dst, phase, 1).wait_recv()

        @pl.when(high)
        def _():
            to_neighbour(src, dst, phase, 0).wait_recv()

    def swap_sent(src, dst, phase):
        @pl.when(high)
        def _():
            to_neighbour(src, dst, phase, 1).wait_send()

        @pl.when(low)
        def _():
            to_neighbour(src, dst, phase, 0).wait_send()

    @pl.when(me == 0)
    def _():
        halo[0:128] = jnp.zeros((128, 128), BF16)
        qhalo[0:64] = jnp.zeros((64, 128), BF16)

    @pl.when(me == n - 1)
    def _():
        halo[128:256] = jnp.zeros((128, 128), BF16)
        qhalo[64:128] = jnp.zeros((64, 128), BF16)

    block = iota((blocks, 128), 0)
    length = dest_ref.shape[1]
    lane = iota((1, 128), 1)
    inner = (lane & 1) * 4 + (lane >> 5)
    rows = iota((16 * n, 128), 0)

    loads[0].wait()

    def targets(source, item):
        wanted = iota((blocks, length), 1) - iota((blocks, length), 0) == source * blocks
        dests = [
            jnp.broadcast_to(
                jnp.sum(jnp.where(wanted, dest_ref[v : v + 1], 0), axis=1, keepdims=True), (blocks, 128)
            )
            for v in range(VES)
        ]
        found = []
        for v in range(VES):
            own = jnp.sum(jnp.where(block == item, dests[v], 0), axis=0, keepdims=True)
            rank = jnp.zeros((blocks, 128), jnp.int32)
            for u in range(VES):
                before = (block <= item) if u < v else (block < item)
                rank = rank + jnp.where(before & (dests[u] == own), 1, 0)
            found.append((own, jnp.sum(rank, axis=0, keepdims=True)))
        return found

    def matches(targets_):
        mask = None
        for target in targets_:
            hit = rows == target
            mask = hit if mask is None else mask | hit
        return onehot(mask)

    item = (iota((blocks, 128), 1) >> 1) % blocks
    picked = matches([own * 16 + rank * 8 + inner for own, rank in targets(me, item)])
    sel[...] = picked.astype(BF16)
    sel_t[...] = picked.T.astype(BF16)
    before = [
        jnp.where((rank == 1) & low, own * 16 + inner, -1) for own, rank in targets(me - 1, item)
    ]
    after = [
        jnp.where((rank == 0) & high, own * 16 + 8 + inner, -1) for own, rank in targets(me + 1, item)
    ]
    sel_h[:, 0:128] = matches(before).astype(BF16)
    sel_h[:, 128:256] = matches(after).astype(BF16)
    item = iota((blocks, 128), 1) % blocks
    comp = (lane // blocks) & 3
    first = [
        jnp.where((rank == 1) & low & (lane < 64), own * 16 + 4 + comp, -1)
        for own, rank in targets(me - 1, item)
    ]
    second = [
        jnp.where((rank == 0) & high & (lane >= 64), own * 16 + 8 + comp, -1)
        for own, rank in targets(me + 1, item)
    ]
    sel_q[...] = matches(first + second).astype(BF16)

    loads[1].wait()
    pl.semaphore_wait(
        barrier, plane + planes - 2 + jnp.where(up_out, 1, 0) + jnp.where(down_out, 1, 0)
    )
    swap(rec_ref, halo, 0)
    for d in range(1, planes):
        greet(entered, (me + d * plane) % n)
    for load in loads[2:]:
        load.wait()

    u = iota((36, 128), 0)
    k = iota((36, 128), 1)
    bias_at = iota((128, 128), 1) - 48
    near = (iota((128, 64), 0) & 63) == iota((128, 64), 1)

    def bias_of(b_ref, at, base):
        values = jnp.sum(jnp.where(near, 0.5 * b_ref[...], 0.0), axis=1, keepdims=True)
        out = base
        for i, piece in enumerate(split3(values)):
            out = out + jnp.where(at == i, piece.astype(F32), 0.0)
        return out

    for g, qs_ in enumerate(GROUPS):
        pair = jnp.concatenate(
            [dot(w_in_ref[...], onehot(u == tap_of(k, q, False), 0.5).astype(BF16), TN) for q in qs_], axis=0
        )
        w1[g] = bias_of(b_in_ref, bias_at, pair).astype(BF16)
        w3[:, 128 * g : 128 * g + 128] = jnp.concatenate(
            [
                dot(onehot(u[:, 0:48] == tap_of(k[:, 0:48], q, True)).astype(BF16), w_out_ref[...], TN)
                for q in qs_
            ],
            axis=1,
        ).astype(BF16)
        if g < 2:
            w2[g] = jnp.concatenate(
                [dot(w_out_ref[...], onehot(u == tap_of(k, q, True), 0.5).astype(BF16), TN) for q in qs_], axis=0
            ).astype(BF16)
    outer = iota((48, 128), 1)
    inside_ = ((outer >= 64) | low) & ((outer < 64) | high)
    w3[:, 256:384] = jnp.where(inside_, w3[:, 256:384].astype(F32), 0.0).astype(BF16)
    wide = onehot((iota((64, 128), 1) & 63) == iota((64, 128), 0), 0.5).astype(BF16)
    half = dot(w_mid_ref[...], wide)
    diagonal = iota((128, 128), 0) >> 6 == iota((128, 128), 1) >> 6
    once = jnp.where(diagonal, jnp.concatenate([half, half], axis=0), 0.0)
    wm[:, 0:128] = once.astype(BF16)
    wm[:, 128:144] = bias_of(b_mid_ref, iota((128, 16), 1), jnp.zeros((128, 16), F32)).astype(BF16)
    wm_t[...] = once.T.astype(BF16)

    sample = iota((128, 128), 1)

    def taps(x):
        x = x.astype(F32)
        left = jnp.where(sample > 0, pltpu.roll(x, 1, 1), 0.0)
        right = jnp.where(sample < 127, pltpu.roll(x, 127, 1), 0.0)
        return jnp.concatenate([left.astype(BF16), x.astype(BF16), right.astype(BF16)], axis=1)

    def spread(choose, source, field, start):
        def step(c, _):
            tiles = dot(choose[pl.ds(pl.multiple_of(c * 128, 128), 128)], source).astype(BF16)
            for t in range(8):
                at = pl.ds(pl.multiple_of((c * 8 + t) * 128, 128), 128)
                for j in range(3):
                    field[start + 16 * j : start + 16 * j + 16, at] = tiles[
                        16 * t : 16 * t + 16, 128 * j : 128 * j + 128
                    ]
            return 0

        lax.fori_loop(0, n // 8, step, 0, unroll=4)

    spread(sel, taps(rec_ref[...]), xs, 0)
    ones = onehot(iota((16, n * 128), 0) < 3).astype(BF16)
    xs[48:64] = ones
    qs[48:64] = jnp.zeros((16, n * 128), BF16)

    size = chunk * 128
    ahead = chunk == n

    def columns(c):
        return pl.ds(0, size) if ahead else pl.ds(pl.multiple_of(c * size, 128), size)

    def loop(body):
        if ahead:
            body(0, 0)
        else:
            lax.fori_loop(0, n // chunk, body, 0)

    const = onehot(iota((16, size), 0) < 3).astype(BF16)

    def activate(h):
        up = 1.0 + jnp.tanh(h)
        return up, h * up

    def slope(up, a):
        return up + a * (2.0 - up)

    def first_layer(g, depth, at):
        return dot(w1[g, :, 0:depth], xs[0:depth, at])

    def mid_layer(a1):
        return dot(wm[...], jnp.concatenate([a1, const], axis=0))

    def inside(c, _):
        at = columns(c)
        up, a = activate(first_layer(0, OWN, at))
        a1 = a.astype(BF16)
        a1s[0, :, at] = a1
        h = mid_layer(a1)
        d1s[0, :, at] = slope(up, a)
        up, a = activate(h)
        a2 = a.astype(BF16)
        a2s[0, :, at] = a2
        if ahead:
            acc[:, at] = dot(w3[:, 0:128], a2)
        d2s[0, :, at] = slope(up, a)
        return 0

    loop(inside)
    for g in (g1, g2, gm):
        g[...] = jnp.zeros_like(g)
    u = iota((48, 128), 0)
    k = iota((48, 128), 1)
    for i, q in enumerate(GROUPS[0] + GROUPS[1]):
        at = slice(128 * i, 128 * i + 128)
        fold1[:, at] = onehot((u == tap_of(k, q, False)) | ((k == 48) & (u == 36))).astype(BF16)
        fold2[:, at] = onehot(u == tap_of(k, q, True)).astype(BF16)
    for i in range(2):
        fold2[:, 512 + 128 * i : 640 + 128 * i] = onehot((k == 0) & (u == 36)).astype(BF16)

    swapped(rec_ref, halo, 0)
    spread(sel_h, jnp.concatenate([taps(halo[0:128]), taps(halo[128:256])], axis=0), xs, OWN)

    small = iota((16, 128), 1)

    def border(c, _):
        at = columns(c)
        h1 = first_layer(1, FIELD, at)
        x1 = first_layer(2, FIELD, at)
        d1s[1, :, at] = h1
        a1 = activate(h1)[1].astype(BF16)
        a1s[1, :, at] = a1
        h2 = mid_layer(a1)
        x2 = mid_layer(activate(x1)[1].astype(BF16))
        d2s[1, :, at] = h2
        a2 = activate(h2)[1].astype(BF16)
        a2s[1, :, at] = a2
        terms = acc[:, at] if ahead else dot(w3[:, 0:128], a2s[0, :, at])
        terms = terms + dot(w3[:, 128:256], a2)
        terms = terms + dot(w3[:, 256:384], activate(x2)[1].astype(BF16))
        for t in range(chunk):
            x = terms[:, 128 * t : 128 * t + 128]
            first = jnp.where(small < 127, pltpu.roll(x[0:16], 127, 1), 0.0)
            last = jnp.where(small > 0, pltpu.roll(x[32:48], 1, 1), 0.0)
            est[c * chunk + t] = (x[16:32] + first + last).astype(BF16)
        return 0

    loop(border)

    residual = dot(sel_t[...], est[...].reshape(16 * n, 128)) - rec_ref[...].astype(F32)
    res_ref[...] = residual
    mine[0:64] = res_ref[pl.ds(0, 64, stride=2)].astype(BF16)
    mine[64:128] = res_ref[pl.ds(1, 64, stride=2)].astype(BF16)
    swap(mine, qhalo, 1)
    spread(sel, taps(residual.astype(BF16)), qs, 0)
    def send(src, dst, phase, peer):
        pltpu.make_async_remote_copy(
            src_ref=src,
            dst_ref=dst,
            send_sem=send_sem.at[phase],
            recv_sem=recv_sem.at[phase],
            device_id={"rec": peer},
            device_id_type=MESH,
        ).start()

    def wait(ref, count, sem):
        every = ref.at[pl.ds(0, count)]
        pltpu.make_async_copy(every, every, sem).wait()

    base = (me // group) * group
    index = me - base
    per = parts.shape[1]
    cut = -(-40 // per)

    def shares(late):
        for i in range(cut) if late else range(cut, group):
            parts[i] = packed[per * i : per * i + per]
        if 2 * cut == group:
            start = 0 if late else cut
            for d in range(cut - 1, 0, -1):
                to = start + ((index % cut) ^ d)
                send(parts.at[to], in4.at[index], 0, base + to)
            rest = [start + index % cut]
        else:
            rest = [index ^ d for d in range(group - 1, 0, -1)]
        for to in rest:
            @pl.when((to != index) & (to < cut if late else to >= cut))
            def _(to=to):
                send(parts.at[to], in4.at[index], 0, base + to)

    def send_mid():
        square = gm[0:64, 0:128] + pltpu.roll(gm[64:128, 0:128], 64, 1)
        packed[40:72] = jnp.where(iota((32, 128), 1) < 64, square[0:32], pltpu.roll(square[32:64], 64, 1))
        packed[72:] = jnp.zeros((packed.shape[0] - 72, 128), F32)
        pl.semaphore_wait(entered, planes - 1)
        shares(False)

    def backward(g, depth):
        def step(c, _):
            at = columns(c)
            row = slice(128 * g, 128 * g + 128)
            field = qs[0:depth, at]
            da2 = dot(w2[g, :, 0:depth], field)
            g2[row, 0:depth] += dot(a2s[g, :, at], field, NT)
            dz2 = (da2 * d2s[g, :, at]).astype(BF16)
            da1 = dot(wm_t[...], dz2)
            gm[:, 0:144] += dot(dz2, jnp.concatenate([a1s[g, :, at], const], axis=0), NT)
            if ahead and g == 1:
                send_mid()
            dz1 = (da1 * d1s[g, :, at]).astype(BF16)
            g1[row, 0:depth] += dot(dz1, xs[0:depth, at], NT)
            return 0

        loop(step)

    def slopes(c, _):
        at = columns(c)
        for d in (d1s, d2s):
            d[1, :, at] = slope(*activate(d[1, :, at]))
        return 0

    backward(0, OWN)
    loop(slopes)
    swapped(mine, qhalo, 1)
    spread(sel_q, taps(qhalo[...]), qs, OWN)
    backward(1, FIELD)
    if not ahead:
        send_mid()

    def folded(fold, pieces):
        total = None
        for piece in split3(jnp.concatenate(pieces, axis=1)):
            term = dot(fold[...], piece, NT)
            total = term if total is None else total + term
        return total

    four = [slice(64 * i, 64 * i + 64) for i in range(4)]
    second = folded(fold2, [g2[at] for at in four] + [gm[0:64, 128:256], gm[64:128, 128:256]])
    first = folded(fold1, [g1[at] for at in four])
    packed[0:40] = jnp.concatenate([first[0:40], second[0:40]], axis=1)
    shares(True)
    in4[index] = parts[index]
    wait(in4, group - 1, recv_sem.at[0])
    part[...] = jnp.sum(in4[...], axis=0, keepdims=True) * scale
    for d in range(n - 1, 0, -1):
        send(part.at[0], in5.at[me], 1, me ^ d)
    in5[me] = part[0]
    wait(in5, n - 1, recv_sem.at[1])
    for i in range(group):
        grad_ref[per * i : per * i + per] = in5[i] + in5[i + group]
    swap_sent(rec_ref, halo, 0)
    swap_sent(mine, qhalo, 1)
    wait(parts, group - 1, send_sem.at[0])
    wait(in5, n - 1, send_sem.at[1])


def deal(res_ref, grad_ref, out_ref, dwi_ref, dbi_ref, dwm_ref, dbm_ref, dwo_ref):
    out_ref[...] = res_ref[...]
    dwi_ref[...] = grad_ref[0:36, 0:64]
    dbi_ref[...] = grad_ref[36:37, 0:64]
    dwm_ref[0:32] = grad_ref[40:72, 0:64]
    dwo_ref[...] = pltpu.roll(grad_ref[0:40], 64, 1)[0:36, 0:64]
    dbm_ref[...] = pltpu.roll(grad_ref[0:40], 64, 1)[36:37, 0:64]
    dwm_ref[32:64] = pltpu.roll(grad_ref[40:72], 64, 1)[:, 0:64]


def local(n, records, dest, w_in, b_in, w_mid, b_mid, w_out):
    parts, blocks, traces, samples = records.shape
    width = n * samples
    group = n // 2
    per = -(-72 // group)
    chunk = n if n <= 32 else 4
    scale = 1.0 / math.sqrt(parts * blocks * n * traces * samples)
    vmem = pl.BlockSpec(memory_space=pltpu.VMEM)
    V = pltpu.VMEM
    hbm = pl.BlockSpec(memory_space=pl.ANY)
    every, share = V((n, per, 128), F32), V((group, per, 128), F32)
    result = pl.pallas_call(
        functools.partial(kernel, n, scale, chunk),
        out_shape=(
            pltpu.VMEM((128, 128), F32),
            pltpu.VMEM((group * per, 128), F32),
        ),
        in_specs=[hbm] * 7,
        out_specs=(vmem,) * 2,
        scratch_shapes=[
            V((128, 128), BF16), V((VES, dest.shape[0]), jnp.int32), V((36, 64), BF16), V((1, 64), F32),
            V((64, 64), BF16), V((1, 64), F32), V((36, 64), BF16),
            V((256, 128), BF16), V((128, 128), BF16), V((128, 128), BF16), V((48, width if chunk == n else 128), F32),
            V((group * per, 128), F32), share, share, V((1, per, 128), F32), every,
            V((16 * n, 128), BF16), V((128, 16 * n), BF16), V((16 * n, 256), BF16),
            V((16 * n, 128), BF16),
            V((3, 128, 128), BF16), V((2, 128, 128), BF16), V((48, 384), BF16),
            V((128, 144), BF16), V((128, 128), BF16), V((48, 512), BF16), V((48, 768), BF16),
            V((FIELD, width), BF16), V((FIELD, width), BF16), V((n, 16, 128), BF16),
            V((2, 128, width), BF16), V((2, 128, width), BF16),
            V((2, 128, width), F32), V((2, 128, width), F32),
            V((256, 128), F32), V((256, 128), F32), V((128, 256), F32),
            pltpu.SemaphoreType.DMA((7,)),
            pltpu.SemaphoreType.DMA((4,)), pltpu.SemaphoreType.DMA((4,)),
            pltpu.SemaphoreType.DMA((2,)), pltpu.SemaphoreType.DMA((2,)),
            pltpu.SemaphoreType.REGULAR,
        ],
        compiler_params=pltpu.CompilerParams(
            collective_id=0, has_side_effects=True, vmem_limit_bytes=63 << 20
        ),
        name="deblend",
    )(
        records.reshape(128, 128), dest.T, w_in.T, b_in.reshape(1, 64), w_mid, b_mid.reshape(1, 64), w_out.T
    )
    residual, dwi, dbi, dwm, dbm, dwo = pl.pallas_call(
        deal,
        out_shape=(
            jax.ShapeDtypeStruct((128, 128), F32),
            jax.ShapeDtypeStruct((36, 64), F32),
            jax.ShapeDtypeStruct((1, 64), F32),
            jax.ShapeDtypeStruct((64, 64), F32),
            jax.ShapeDtypeStruct((1, 64), F32),
            jax.ShapeDtypeStruct((36, 64), F32),
        ),
        in_specs=[vmem] * 2,
        out_specs=(vmem,) * 6,
        name="deal",
    )(*[pltpu.with_memory_space_constraint(x, pltpu.VMEM) for x in result])
    return (
        residual.reshape(records.shape),
        dwi.T,
        dbi.reshape(64),
        dwm,
        dbm.reshape(64),
        dwo.T,
    )


def solution(mesh):
    return jax.shard_map(
        functools.partial(local, mesh.shape["rec"]),
        mesh=mesh,
        in_specs=(
            P(None, ("groups", "rec"), None, None),
            P("groups", None),
            P(),
            P(),
            P(),
            P(),
            P(),
        ),
        out_specs=(
            P(None, ("groups", "rec"), None, None),
            P("groups", None),
            P("groups"),
            P("groups", None),
            P("groups"),
            P("groups", None),
        ),
        check_vma=False,
    )
```
